32 devices in a mesh: rows: 16 (over z, y, x), cols: 2 (over core).
Axes of the slice: x: 2, y: 2, z: 4, core: 2. Of those that a mesh axis runs over, the one named last changes fastest.
Arguments:
- iterate: bfloat16 [24576, 512], P('rows', 'cols'), may hold values from -256 to 256, as said below
- residual: bfloat16 [24576, 512], P('rows', 'cols'), may hold values from -256 to 256, as said below
- leaf_offset: bfloat16 [24576, 768], P('rows', 'cols'), may hold values from -0.109375 to 0.109375
- bases_v: bfloat16 [5, 24576, 256], P(None, 'rows', 'cols'), may hold values from -1 to 1, as said below
- bases_u: bfloat16 [5, 24576, 256], P(None, 'rows', 'cols'), may hold values from -0.1875 to 0.1875
- estimate: float32 [512], P('cols'), may hold values from -1 to 1
Outputs:
- updated: float32 [24576, 512], P('rows', 'cols')
- functional: float32 [512], P('cols')
The draws below stay inside these ranges and needn't reach their ends.
Inputs may be any that keep to these rules, and one draw needn't show every extreme that they name: Entries of the iterate, real valued. Entries of the residual, real valued. `bases_v`: real valued basis entries.
All inputs are finite; a program needn't handle non-finite values.
Results may differ from the reference program's by a relative error of at most 0.0085.
Values may be sent and summed in bfloat16 or wider, within the bound.
A program may use at most 64 MiB of HBM per device.

```python
import jax
import jax.numpy as jnp
from jax import lax

R = 256
VECS = 512
ROWS = 1536
LEAF = 768
LEVELS = 4
TREE = 5
TOTAL = 24576


def shared_parts(key):
    keys = jax.random.split(jax.random.fold_in(key, 29), 5)
    block_count = TOTAL // ROWS
    roughness = 10.0 ** (0.6 * jax.random.uniform(keys[0], (block_count, ROWS, 1), dtype=jnp.float32) - 0.3)
    column_scale = 2.0 ** (2.0 * jax.random.uniform(keys[1], (1, 1, VECS), dtype=jnp.float32) - 1.0)
    amplitude = 10.0 ** (1.5 * jax.random.uniform(keys[2], (block_count, 1, VECS), dtype=jnp.float32) - 0.75)
    coupling = jax.random.uniform(keys[3], (block_count, 1, VECS), dtype=jnp.float32, minval=-1.0, maxval=1.0)
    common_field = jnp.clip(jax.random.normal(keys[4], (block_count, ROWS, VECS), dtype=jnp.float32), -3.5, 3.5)
    return (common_field, coupling, roughness * amplitude * column_scale)


def private_field(key, salt):
    keys = jax.random.split(jax.random.fold_in(key, salt), 1)
    block_count = TOTAL // ROWS
    return jnp.clip(jax.random.normal(keys[0], (block_count, ROWS, VECS), dtype=jnp.float32), -3.5, 3.5)


def draw_iterate(key, part):
    common_field, coupling, scale = shared_parts(key)
    values = (private_field(key, 11) + common_field) * scale
    return values.reshape(TOTAL, VECS).astype(jnp.bfloat16)


def draw_residual(key, part):
    common_field, coupling, scale = shared_parts(key)
    values = (private_field(key, 17) + 2.0 * coupling * common_field) * scale
    return values.reshape(TOTAL, VECS).astype(jnp.bfloat16)


def draw_bases_v(key, part):
    basis_key = jax.random.fold_in(key, 23)
    depth = jnp.arange(TREE, dtype=jnp.float32)
    level_scale = jnp.sqrt(2.0 ** depth / TOTAL)[:, None, None]
    values = jnp.clip(jax.random.normal(basis_key, (TREE, TOTAL, R), dtype=jnp.float32), -4.0, 4.0)
    return (values * level_scale).astype(jnp.bfloat16)


def shard_levels(rng, dims, shards, smallest, top_value):
    def one(position, blocks):
        heights = jax.random.uniform(jax.random.fold_in(jax.random.fold_in(rng, 6), position), (blocks,), jnp.float32, smallest / len(shards), top_value / len(shards))
        return jnp.repeat(jnp.exp(heights), dims[position] // blocks).reshape((-1,) + (1,) * (len(dims) - position - 1))

    factor_of = one(*shards[0])
    for cut in shards[1:]:
        factor_of = factor_of * one(*cut)
    return factor_of


def centred(own_key, extent, deviation, most, cuts=(), kind=jnp.bfloat16):
    values = jax.random.normal(own_key, extent, jnp.float32) * deviation
    if len(cuts) > 0:
        values = shard_levels(own_key, extent, cuts, -0.22, 0.18) * values
    return jnp.clip(values, min=-most, max=most).astype(kind)


def setup_inputs(seed: int = 0) -> dict:
    key_of = jax.random.split(jax.random.key(seed), 7)
    iterate = draw_iterate(jax.random.fold_in(key_of[6], 71), 0)
    residual = draw_residual(jax.random.fold_in(key_of[6], 71), 0)
    leaf_offset = centred(key_of[2], (TOTAL, LEAF), (4 * LEAF) ** -0.5, 0.109375, ((0, 16), (1, 2)))
    bases_v = draw_bases_v(jax.random.fold_in(key_of[6], 71), 0)
    bases_u = centred(key_of[4], (TREE, TOTAL, R), (4 * R) ** -0.5, 0.1875, ((1, 16), (2, 2)))
    estimate = jnp.clip(jax.random.uniform(key_of[5], (VECS,), jnp.float32, -1.0, 1.0) * shard_levels(key_of[5], (VECS,), ((0, 2),), -0.4, 0.0), -1.0, 1.0)
    return {"iterate": iterate, "residual": residual, "leaf_offset": leaf_offset, "bases_v": bases_v, "bases_u": bases_u, "estimate": estimate}


epsilon = 1e-6


def leaf_product(paired):
    return jnp.dot(paired[0], paired[1], preferred_element_type=jnp.float32)


def project_node(paired):
    return lax.dot_general(paired[0], paired[1], (((0,), (0,)), ((), ())), preferred_element_type=jnp.float32)


def reference(iterate, residual, leaf_offset, bases_v, bases_u, estimate):
    leaf_count = TOTAL // LEAF
    residual_blocks = residual.reshape(leaf_count, LEAF, VECS)
    offset_blocks = leaf_offset.reshape(leaf_count, LEAF, LEAF)
    leaf_terms = lax.map(leaf_product, (offset_blocks, residual_blocks))
    current = residual.astype(jnp.float32) + leaf_terms.reshape(TOTAL, VECS)
    for level_index in range(LEVELS, -1, -1):
        node_count = 2 ** level_index
        node_rows = TOTAL // node_count
        rounded = current.astype(jnp.bfloat16).reshape(node_count, node_rows, VECS)
        right_nodes = bases_v[level_index].reshape(node_count, node_rows, R)
        coefficients = lax.map(project_node, (right_nodes, rounded))
        narrow = coefficients.astype(jnp.bfloat16)
        left_nodes = bases_u[level_index].reshape(node_count, node_rows, R)
        correction = lax.map(leaf_product, (left_nodes, narrow))
        current = current - correction.reshape(TOTAL, VECS)
    updated = iterate.astype(jnp.float32) - current
    numerator = jnp.sum(updated * residual.astype(jnp.float32), axis=0)
    denominator = jnp.sum(updated * updated, axis=0)
    functional = estimate + numerator / (denominator + epsilon)
    return updated, functional
```

```python
import functools

import jax
import jax.numpy as jnp
from jax import lax
from jax.experimental import pallas as pl
from jax.experimental.pallas import tpu as pltpu
from jax.sharding import PartitionSpec as P

epsilon = 1e-06
MESH = pl.DeviceIdType.MESH
MOST = 16


def log2(value):
    return value.bit_length() - 1


def tdot(a, b):
    return lax.dot_general(a, b, (((0,), (0,)), ((), ())), preferred_element_type=jnp.float32)


def dot(a, b):
    return jnp.dot(a, b, preferred_element_type=jnp.float32)


def pairs_of(low):
    return [(l, k) for k in range(1, low) for l in range(k)]


def kernel(n, it_h, r_h, leaf_h, v_h, u_h, est_h, out, fun,
           it, r, rp, leaf, v, u, est, x, ws, wr, s, wx, wy, w3, p, ps3, rs3, gs, gr, c, gx, gy,
           st, sg, sx, lsem, ssem, rsem, hs, go):
    bf, f32 = jnp.bfloat16, jnp.float32
    rows, vecs = r.shape
    rank = v.shape[2]
    half = rank // 2
    width = leaf.shape[1]
    lh = width // 2
    top = log2(n)
    low = top - 1
    pairs = pairs_of(low)
    most = min(n, MOST)
    me = lax.axis_index("rows")
    col = lax.axis_index("cols")
    other = 1 - col
    mine = pl.ds(pl.multiple_of(col * half, half), half)

    used = {"l": 0, "s": 0}

    def fetch(src, dst):
        copy = pltpu.make_async_copy(src, dst, lsem.at[used["l"]])
        used["l"] += 1
        copy.start()
        return copy

    got_v, got_u = {}, {}

    def fetch_v(l):
        got_v[l] = fetch(v_h.at[l], v.at[l, :, mine])

    def fetch_u(l):
        got_u[l] = fetch(u_h.at[l], u.at[l, :, mine])

    for l in range(low - 1):
        fetch_v(l)
    for l in range(1, low):
        fetch_u(l)
    got_r = [fetch(r_h, r)]
    for k in range(rows // width):
        for part, which in enumerate((col, other)):
            start = pl.multiple_of(k * width + which * lh, 16)
            got_r.append(fetch(r_h.at[pl.ds(start, lh)], rp.at[pl.ds(k * width + part * lh, lh)]))
    got_leaf = fetch(leaf_h, leaf.at[:, pl.ds(0, lh)])
    for l in (top, top - 1):
        fetch_v(l)
        fetch_u(l)
    fetch_v(low - 1)
    fetch_u(0)
    got_it = fetch(it_h, it)
    got_est = fetch(est_h, est)

    barrier = pltpu.get_barrier_semaphore()
    peers = list(range(1, most)) + [most << b for b in range(log2(n // most))]

    @pl.when(col == 1)
    def _():
        pl.semaphore_signal(barrier, inc=1, device_id={"cols": other}, device_id_type=MESH)

    @pl.when(col == 0)
    def _():
        pl.semaphore_wait(barrier, 1)
        pl.semaphore_signal(hs, inc=1, device_id={"cols": other}, device_id_type=MESH)

    @pl.when(col == 1)
    def _():
        pl.semaphore_wait(hs, 1)
        for o in peers:
            pl.semaphore_signal(barrier, inc=1, device_id={"rows": me ^ o}, device_id_type=MESH)

    sent = []

    def await_bytes(ref, sem):
        pltpu.make_async_copy(ref, ref, sem).wait()

    def slot():
        used["s"] += 1
        return used["s"] - 1

    def push(src, dst, to=None, at=None):
        at = slot() if at is None else at
        copy = pltpu.make_async_remote_copy(
            src_ref=src, dst_ref=dst, send_sem=ssem.at[at], recv_sem=rsem.at[at],
            device_id={"cols": other} if to is None else {"rows": to}, device_id_type=MESH)
        copy.start()
        return copy

    def lone(src, dst, to=None):
        copy = push(src, dst, to)
        sent.append(copy.wait_send)
        return copy

    in_v, in_u = {}, {}

    def push_v(l):
        in_v[l] = lone(v_h.at[l], v.at[l, :, mine])

    def push_u(l):
        in_u[l] = lone(u_h.at[l], u.at[l, :, mine])

    for l in range(low - 1):
        push_v(l)
    in_leaf = lone(leaf_h, leaf.at[:, pl.ds(lh, lh)])
    push_v(top)
    push_u(top)
    push_v(top - 1)
    push_v(low - 1)
    push_u(top - 1)
    for l in range(low - 1, -1, -1):
        push_u(l)

    def ready(l, got, come):
        if l in got:
            got.pop(l).wait()
        come[l].wait_recv()

    def scatter(src, dst, group):
        h = min(group, most)
        ch = rank // h
        j = me & (h - 1)
        at = slot()
        for o in range(h - 1, 0, -1):
            push(src(pl.ds(pl.multiple_of((j ^ o) * ch, 16), ch)), dst(pl.ds((o - 1) * ch, ch)), me ^ o, at)
        whole = dst(pl.ds(0, (h - 1) * ch))
        sent.append(lambda: await_bytes(whole, ssem.at[at]))
        return lambda: await_bytes(whole, rsem.at[at])

    def gather(ref, group):
        h = min(group, most)
        ch = rank // h
        share = pl.ds(pl.multiple_of((me & (h - 1)) * ch, 16), ch)
        at = slot()
        for o in range(h - 1, 0, -1):
            push(ref(share), ref(share), me ^ o, at)
        whole = ref(pl.ds(0, (h - 1) * ch))
        sent.append(lambda: await_bytes(whole, ssem.at[at]))
        return lambda: await_bytes(whole, rsem.at[at])

    def total_of(src, come, away, back, group):
        h = min(group, most)
        ch = rank // h
        share = pl.ds(pl.multiple_of((me & (h - 1)) * ch, 16), ch)
        total = src(share)[...].astype(f32)
        for o in range(1, h):
            total = total + come(pl.ds((o - 1) * ch, ch))[...].astype(f32)
        for b in range(log2(group // h)):
            away(b)[...] = total
            lone(away(b), back(b), me ^ (most << b)).wait_recv()
            total = total + back(b)[...]
        return share, total

    group_of = [2 ** (top - l) for l in range(low)]

    for copy in got_r:
        copy.wait()
    got_leaf.wait()
    leaves = rows // width
    for k in range(leaves):
        b = pl.ds(k * width, width)
        x[b] = r[b].astype(f32) + dot(leaf[b, pl.ds(0, lh)], rp[pl.ds(k * width, lh)])

    for l in range(low - 1):
        ready(l, got_v, in_v)
    for k in range(1, low):
        got_u.pop(k).wait()
    for i, (l, k) in enumerate(pairs):
        ws[i] = tdot(v[l], u[k, :, mine]).astype(bf)

    @pl.when(col == 1)
    def _():
        pl.semaphore_wait(barrier, len(peers))
        pl.semaphore_signal(go, inc=1, device_id={"cols": other}, device_id_type=MESH)

    @pl.when(col == 0)
    def _():
        pl.semaphore_wait(go, 1)

    come_w = [
        scatter(lambda d, i=i: ws.at[i, d], lambda d, i=i: wr.at[i, d], group_of[k])
        for i, (l, k) in enumerate(pairs)
    ]

    in_leaf.wait_recv()
    for k in range(leaves):
        b = pl.ds(k * width, width)
        x[b] = x[b] + dot(leaf[b, pl.ds(lh, lh)], rp[pl.ds(k * width + lh, lh)])
    ready(top, got_v, in_v)
    narrow = tdot(v[top], x[...].astype(bf)).astype(bf)
    ready(top, got_u, in_u)
    x[...] = x[...] - dot(u[top], narrow)
    ready(top - 1, got_v, in_v)
    partial = tdot(v[top - 1], x[...].astype(bf))
    ps3[...] = partial.astype(bf)
    in_pair = lone(ps3, rs3, me ^ 1)

    come_s = []
    for i, (l, k) in enumerate(pairs):
        come_w[i]()
        share, total = total_of(
            lambda d: ws.at[i, d], lambda d: wr.at[i, d], lambda b: wx.at[i, b, pl.ds(0, rank // most)],
            lambda b: wy.at[i, b, pl.ds(0, rank // most)], group_of[k])
        s[i, share, mine] = total.astype(bf)
        come_s.append(gather(lambda d, i=i: s.at[i, d, mine], group_of[k]))

    ready(low - 1, got_v, in_v)
    for l in range(low - 1, -1, -1):
        p[l] = tdot(v[l], x[...].astype(bf))
    ready(top - 1, got_u, in_u)
    for l in range(low - 1, -1, -1):
        w3[l] = tdot(v[l], u[top - 1]).astype(bf)
    in_pair.wait_recv()
    c3 = (partial + rs3[...].astype(f32)).astype(bf)
    for l in range(low - 1, -1, -1):
        p[l] = p[l] - dot(w3[l], c3)
    gs[low - 1] = p[low - 1].astype(bf)
    come_g = {}

    def send_g(l):
        come_g[l] = scatter(lambda d: gs.at[l, d], lambda d: gr.at[l, d], group_of[l])

    send_g(low - 1)
    in_s = []
    for i in range(len(pairs)):
        come_s[i]()
        in_s.append(lone(s.at[i, :, mine], s.at[i, :, mine]))
    got_it.wait()
    out[...] = it[...].astype(f32) - x[...] + dot(u[top - 1], c3)
    for copy in in_s:
        copy.wait_recv()
    for l in range(low - 2, -1, -1):
        value = p[l]
        for k in range(low - 1, l, -1):
            value = value - dot(s[pairs.index((l, k))], gs[k])
        gs[l] = value.astype(bf)
        send_g(l)

    come_c = {}
    for l in range(low - 1, -1, -1):
        come_g[l]()
        share, total = total_of(
            lambda d: gs.at[l, d], lambda d: gr.at[l, d], lambda b: gx.at[l, b], lambda b: gy.at[l, b], group_of[l])
        c[l, share] = total.astype(bf)
        come_c[l] = gather(lambda d, l=l: c.at[l, d], group_of[l])
    for l in range(low - 1, 0, -1):
        ready(l, got_u, in_u)
        come_c[l]()
        out[...] = out[...] + dot(u[l], c[l])
    ready(0, got_u, in_u)
    come_c[0]()

    num = jnp.zeros((1, vecs), f32)
    den = jnp.zeros((1, vecs), f32)
    blocks = 4
    size = rows // blocks
    for k in range(blocks):
        b = pl.ds(k * size, size)
        updated = out[b] + dot(u[0, b], c[0])
        out[b] = updated
        num = num + jnp.sum(updated * r[b].astype(f32), axis=0, keepdims=True)
        den = den + jnp.sum(updated * updated, axis=0, keepdims=True)
    st[pl.ds(0, 1)] = num
    st[pl.ds(1, 1)] = den
    at = slot()
    for o in range(most - 1, 0, -1):
        push(st, sg.at[o - 1], me ^ o, at)
    sent.append(lambda: await_bytes(sg, ssem.at[at]))
    got_est.wait()
    await_bytes(sg, rsem.at[at])
    total = st[...]
    for o in range(1, most):
        total = total + sg[o - 1]
    for b in range(log2(n // most)):
        sx[0, b] = total
        lone(sx.at[0, b], sx.at[1, b], me ^ (most << b)).wait_recv()
        total = total + sx[1, b]
    fun[...] = (est[...] + total[0:1] / (total[1:2] + epsilon)).reshape(vecs)
    for done in sent:
        done()


def per_device(n, iterate, residual, leaf_offset, bases_v, bases_u, estimate):
    rows, vecs = residual.shape
    levels = bases_v.shape[0]
    rank = 2 * bases_v.shape[2]
    width = 2 * leaf_offset.shape[1]
    half = rank // 2
    top = levels - 1
    low = top - 1
    count = len(pairs_of(low))
    most = min(n, MOST)
    far = log2(n // most)
    room = max(far, 1)
    slots = 2 * levels + 1 + 3 * count + 2 * low + 2 + far * (count + low + 1)
    hbm = pl.BlockSpec(memory_space=pl.ANY)
    vmem = pl.BlockSpec(memory_space=pltpu.VMEM)
    bf, f32 = jnp.bfloat16, jnp.float32
    args = (iterate, residual, leaf_offset, bases_v, bases_u, estimate.reshape(1, vecs))
    updated, functional = pl.pallas_call(
        functools.partial(kernel, n),
        out_shape=(
            jax.ShapeDtypeStruct((rows, vecs), f32),
            jax.ShapeDtypeStruct((vecs,), f32),
        ),
        in_specs=[hbm] * 6,
        out_specs=(vmem, vmem),
        scratch_shapes=[
            pltpu.VMEM((rows, vecs), bf),
            pltpu.VMEM((rows, vecs), bf),
            pltpu.VMEM((rows, vecs), bf),
            pltpu.VMEM((rows, width), bf),
            pltpu.VMEM((levels, rows, rank), bf),
            pltpu.VMEM((levels, rows, rank), bf),
            pltpu.VMEM((1, vecs), f32),
            pltpu.VMEM((rows, vecs), f32),
            pltpu.VMEM((count, rank, half), bf),
            pltpu.VMEM((count, rank, half), bf),
            pltpu.VMEM((count, rank, rank), bf),
            pltpu.VMEM((count, room, rank // most, half), f32),
            pltpu.VMEM((count, room, rank // most, half), f32),
            pltpu.VMEM((low, rank, rank), bf),
            pltpu.VMEM((low, rank, vecs), f32),
            pltpu.VMEM((rank, vecs), bf),
            pltpu.VMEM((rank, vecs), bf),
            pltpu.VMEM((low, rank, vecs), bf),
            pltpu.VMEM((low, rank, vecs), bf),
            pltpu.VMEM((low, rank, vecs), bf),
            pltpu.VMEM((low, room, rank // most, vecs), f32),
            pltpu.VMEM((low, room, rank // most, vecs), f32),
            pltpu.VMEM((2, vecs), f32),
            pltpu.VMEM((most - 1, 2, vecs), f32),
            pltpu.VMEM((2, room, 2, vecs), f32),
            pltpu.SemaphoreType.DMA((2 * levels + 2 * (rows // width) + 4,)),
            pltpu.SemaphoreType.DMA((slots,)),
            pltpu.SemaphoreType.DMA((slots,)),
            pltpu.SemaphoreType.REGULAR,
            pltpu.SemaphoreType.REGULAR,
        ],
        compiler_params=pltpu.CompilerParams(
            collective_id=0, has_side_effects=True, vmem_limit_bytes=40 << 20
        ),
    )(*(pltpu.with_memory_space_constraint(a, pltpu.HBM) for a in args))
    return updated, functional


def solution(mesh):
    return jax.shard_map(
        functools.partial(per_device, mesh.shape["rows"]),
        mesh=mesh,
        in_specs=(
            P("rows", "cols"),
            P("rows", "cols"),
            P("rows", "cols"),
            P(None, "rows", "cols"),
            P(None, "rows", "cols"),
            P("cols"),
        ),
        out_specs=(P("rows", "cols"), P("cols")),
        check_vma=False,
    )
```

```python
import functools

import jax
import jax.numpy as jnp
from jax import lax
from jax.experimental import pallas as pl
from jax.experimental.pallas import tpu as pltpu
from jax.sharding import PartitionSpec as P

epsilon = 1e-06
MESH = pl.DeviceIdType.MESH
MOST = 16


def log2(value):
    return value.bit_length() - 1


def tdot(a, b):
    return lax.dot_general(a, b, (((0,), (0,)), ((), ())), preferred_element_type=jnp.float32)


def dot(a, b):
    return jnp.dot(a, b, preferred_element_type=jnp.float32)


def shares(n, levels, rank, which, most):
    found, start = [], 0
    for level, many in which:
        h = min(2 ** (levels - 1 - level), most)
        found.append((level, h, rank // h, many, start))
        start += many * (rank // h)
    return found, start


def classes_of(found):
    out, low = [], 0
    for level, h, ch, many, start in reversed(found):
        if h > low:
            out.append((low, h, start + many * ch))
            low = h
    return out


def crosses(n, levels, rank):
    return shares(n, levels, rank, [(k, k) for k in range(1, levels - 2)], MOST)


def sums(n, levels, rank):
    return shares(n, levels, rank, [(l, 1) for l in range(levels - 3)], MOST)


def scratch_of(n, levels, rows, rank, vecs, width):
    half, top = rank // 2, levels - 1
    low = top - 1
    most = min(n, MOST)
    room = max(log2(n // most), 1)
    bf, f32 = jnp.bfloat16, jnp.float32
    sh = min(n // 2, MOST)
    _, cross_rows = crosses(n, levels, rank)
    _, sum_rows = sums(n, levels, rank)
    return [
        ("it", bf, (rows, vecs)),
        ("r", bf, (rows, vecs)),
        ("rp", bf, (rows, vecs)),
        ("leaf", bf, (rows, width)),
        ("v", bf, (levels, rows, rank)),
        ("u", bf, (levels, rows, rank)),
        ("est", f32, (1, vecs)),
        ("x", f32, (rows, vecs)),
        ("w3", bf, (low, rank, rank)),
        ("p", f32, (low, rank, vecs)),
        ("ps3", bf, (rank, vecs)),
        ("rs3", bf, (rank, vecs)),
        ("g2", bf, (rank, vecs)),
        ("gr2", bf, (rank, vecs)),
        ("c2", bf, (rank, vecs)),
        ("gs", bf, (most, sum_rows, vecs)),
        ("gr", bf, (most, sum_rows, vecs)),
        ("c", bf, (most, sum_rows, vecs)),
        ("gx", f32, (low, room, rank // most, vecs)),
        ("gy", f32, (low, room, rank // most, vecs)),
        ("ws", bf, (sh, cross_rows, half)),
        ("wr", bf, (2, sh, cross_rows, half)),
        ("s", bf, (sh, cross_rows, rank)),
        ("wx", f32, (room, cross_rows, rank)),
        ("wy", f32, (room, cross_rows, rank)),
        ("st", f32, (2, vecs)),
        ("sg", f32, (most - 1, 2, vecs)),
        ("sx", f32, (2, room, 2, vecs)),
    ]


def kernel(n, names, it_h, r_h, leaf_h, v_h, u_h, est_h, out, fun, *refs):
    buf = dict(zip(names, refs))
    lsem, ssem, rsem, hs, go, go_node, near, go_all = refs[len(names):]
    it, r, rp, leaf, v, u, est, x = (buf[a] for a in ("it", "r", "rp", "leaf", "v", "u", "est", "x"))
    w3, p, ps3, rs3, g2, gr2, c2 = (buf[a] for a in ("w3", "p", "ps3", "rs3", "g2", "gr2", "c2"))
    gs, gr, c, gx, gy, ws, wr, s, wx, wy = (
        buf[a] for a in ("gs", "gr", "c", "gx", "gy", "ws", "wr", "s", "wx", "wy"))
    st, sg, sx = (buf[a] for a in ("st", "sg", "sx"))
    bf, f32 = jnp.bfloat16, jnp.float32
    rows, vecs = r.shape
    levels, _, rank = v.shape
    half = rank // 2
    width = leaf.shape[1]
    lh = width // 2
    leaves = rows // width
    top = levels - 1
    low = top - 1
    most = min(n, MOST)
    sh = min(n // 2, MOST)
    me = lax.axis_index("rows")
    col = lax.axis_index("cols")
    other = 1 - col
    mine = pl.ds(pl.multiple_of(col * half, half), half)
    in_node = me & (sh - 1)
    in_all = me & (most - 1)
    group_of = [2 ** (top - l) for l in range(levels)]

    def signal(sem, to=None, core=None):
        device = {} if to is None else {"rows": to}
        if core is not None:
            device["cols"] = core
        pl.semaphore_signal(sem, inc=1, device_id=device, device_id_type=MESH)

    barrier = pltpu.get_barrier_semaphore()
    partners = [1] + [1 << b for b in range(log2(sh), log2(n))]

    @pl.when(col == 1)
    def _():
        signal(barrier, core=0)
        for o in range(sh - 1, 1, -1):
            signal(barrier, me ^ o)

    used = {"l": 0, "s": 0}

    def fetch(src, dst):
        copy = pltpu.make_async_copy(src, dst, lsem.at[used["l"]])
        used["l"] += 1
        copy.start()
        return copy

    got_v, got_u = {}, {}

    def fetch_v(l):
        got_v[l] = fetch(v_h.at[l], v.at[l, :, mine])

    def fetch_u(l):
        got_u[l] = fetch(u_h.at[l], u.at[l, :, mine])

    for l in range(low - 1):
        fetch_v(l)
        fetch_u(l + 1)

    @pl.when(col == 0)
    def _():
        pl.semaphore_wait(barrier, 1)
        signal(hs, core=1)

    @pl.when(col == 1)
    def _():
        pl.semaphore_wait(hs, 1)
        for o in partners:
            signal(barrier, me ^ o)

    sent = []

    def await_bytes(ref, sem):
        pltpu.make_async_copy(ref, ref, sem).wait()

    def slot(many=1):
        used["s"] += many
        return used["s"] - many

    def push(src, dst, to=None, at=None, core=None):
        at = slot() if at is None else at
        device = {} if to is None else {"rows": to}
        if to is None or core is not None:
            device["cols"] = other if core is None else core
        copy = pltpu.make_async_remote_copy(
            src_ref=src, dst_ref=dst, send_sem=ssem.at[at], recv_sem=rsem.at[at],
            device_id=device, device_id_type=MESH)
        copy.start()
        return copy

    def lone(src, dst, to=None):
        copy = push(src, dst, to)
        sent.append((None, copy.wait_send))
        return copy

    in_v, in_u = {}, {}

    def push_v(l):
        in_v[l] = lone(v_h.at[l], v.at[l, :, mine])

    def push_u(l):
        in_u[l] = lone(u_h.at[l], u.at[l, :, mine])

    for l in range(low - 1):
        push_v(l)
    got_r = [fetch(r_h, r)]
    for k in range(leaves):
        for part, which in enumerate((col, other)):
            start = pl.multiple_of(k * width + which * lh, 16)
            got_r.append(fetch(r_h.at[pl.ds(start, lh)], rp.at[pl.ds(k * width + part * lh, lh)]))
    got_leaf = fetch(leaf_h, leaf.at[:, pl.ds(0, lh)])
    in_leaf = lone(leaf_h, leaf.at[:, pl.ds(lh, lh)])
    for l in (top, top - 1):
        fetch_v(l)
        push_v(l)
        fetch_u(l)
        push_u(l)
    fetch_v(low - 1)
    push_v(low - 1)
    fetch_u(0)
    for l in range(low - 1, -1, -1):
        push_u(l)
    got_it = fetch(it_h, it)
    got_est = fetch(est_h, est)

    def ready(l, got, come):
        if l in got:
            got.pop(l).wait()
        come[l].wait_recv()

    def scatter(src, dst, group):
        h = min(group, most)
        ch = rank // h
        j = me & (h - 1)
        at = slot()
        for o in range(h - 1, 0, -1):
            push(src.at[pl.ds(pl.multiple_of((j ^ o) * ch, 16), ch)], dst.at[pl.ds((o - 1) * ch, ch)], me ^ o, at)
        whole = dst.at[pl.ds(0, (h - 1) * ch)]
        sent.append((None, lambda: await_bytes(whole, ssem.at[at])))
        return lambda: await_bytes(whole, rsem.at[at])

    def gather(ref, group):
        h = min(group, most)
        ch = rank // h
        share = pl.ds(pl.multiple_of((me & (h - 1)) * ch, 16), ch)
        at = slot()
        for o in range(h - 1, 0, -1):
            push(ref.at[share], ref.at[share], me ^ o, at)
        whole = ref.at[pl.ds(0, (h - 1) * ch)]
        sent.append((None, lambda: await_bytes(whole, ssem.at[at])))
        return lambda: await_bytes(whole, rsem.at[at])

    def total_of(own, come, away, back, group):
        h = min(group, most)
        total = own.astype(f32)
        for o in range(1, h):
            total = total + come(o).astype(f32)
        for b in range(log2(group // h)):
            away.at[b][...] = total
            lone(away.at[b], back.at[b], me ^ (most << b)).wait_recv()
            total = total + back[b]
        return total

    def first_of(j, h):
        return j - (j & (h - 1))

    for copy in got_r:
        copy.wait()
    got_leaf.wait()
    for k in range(leaves):
        b = pl.ds(k * width, width)
        x[b] = r[b].astype(f32) + dot(leaf[b, pl.ds(0, lh)], rp[pl.ds(k * width, lh)])

    found, _ = crosses(n, levels, rank)
    kinds = classes_of(found)
    for k, h, ch, many, start in found:
        got_u.pop(k).wait()
        ready(k - 1, got_v, in_v)
        for l in range(many):
            ws[pl.ds(first_of(in_node, h), h), pl.ds(start + l * ch, ch)] = (
                tdot(v[l], u[k, :, mine]).astype(bf).reshape(h, ch, half))

    @pl.when(col == 1)
    def _():
        pl.semaphore_wait(barrier, sh - 2 + len(partners))
        signal(go, core=0)

    @pl.when(col == 0)
    def _():
        pl.semaphore_wait(go, 1)

    to_w = [slot(2) for _ in kinds]
    to_s = [slot() for _ in kinds]
    to_other = [slot() for _ in kinds]
    for (lo, hi, count), at in reversed(list(zip(kinds, to_w))):
        part = pl.ds(0, count)
        for o in range(hi - 1, max(lo, 1) - 1, -1):
            push(ws.at[in_node ^ o, part], wr.at[col, o, part], me ^ o, at + col, 1)
        if lo == 0:

            @pl.when(col == 0)
            def _():
                push(ws.at[in_node, part], wr.at[0, 0, part], me, at, 1)

        a, b = ws.at[pl.ds(0, hi - lo), part], ws.at[pl.ds(0, hi - max(lo, 1)), part]
        sent.append((0, lambda a=a, at=at: await_bytes(a, ssem.at[at])))
        sent.append((1, lambda b=b, at=at: await_bytes(b, ssem.at[at + 1])))

    in_leaf.wait_recv()
    for k in range(leaves):
        b = pl.ds(k * width, width)
        x[b] = x[b] + dot(leaf[b, pl.ds(lh, lh)], rp[pl.ds(k * width + lh, lh)])
    ready(top, got_v, in_v)
    narrow = tdot(v[top], x[...].astype(bf)).astype(bf)
    ready(top, got_u, in_u)
    x[...] = x[...] - dot(u[top], narrow)
    ready(top - 1, got_v, in_v)
    partial = tdot(v[top - 1], x[...].astype(bf))
    ps3[...] = partial.astype(bf)
    in_pair = lone(ps3, rs3, me ^ 1)

    far_at = {(k, b): slot() for k, h, _, _, _ in found for b in range(log2(group_of[k] // h))}

    @pl.when(col == 1)
    def _():
        for (lo, hi, count), at in zip(kinds, to_w):
            await_bytes(wr.at[0, pl.ds(lo, hi - lo), pl.ds(0, count)], rsem.at[at])
            await_bytes(wr.at[1, pl.ds(max(lo, 1), hi - max(lo, 1)), pl.ds(0, count)], rsem.at[at + 1])
        for k, h, ch, many, start in found:
            part = pl.ds(start, many * ch)
            first, second = wr[0, 0, part].astype(f32), ws[in_node, part].astype(f32)
            for o in range(1, h):
                first = first + wr[0, o, part].astype(f32)
                second = second + wr[1, o, part].astype(f32)
            for b in range(log2(group_of[k] // h)):
                wx[b, part, pl.ds(0, half)] = first
                wx[b, part, pl.ds(half, half)] = second
                push(wx.at[b, part], wy.at[b, part], me ^ (most << b), far_at[k, b]).wait_recv()
                first = first + wy[b, part, pl.ds(0, half)]
                second = second + wy[b, part, pl.ds(half, half)]
            s[in_node, part, pl.ds(0, half)] = first.astype(bf)
            s[in_node, part, pl.ds(half, half)] = second.astype(bf)
        for (lo, hi, count), at in reversed(list(zip(kinds, to_s))):
            share = s.at[in_node, pl.ds(0, count)]
            for o in range(hi - 1, max(lo, 1) - 1, -1):
                push(share, share, me ^ o, at)
        signal(go_node, core=0)
        if sh < most:
            signal(near, me ^ sh)

    for (lo, hi, count), at, to in zip(kinds, to_s, to_other):
        a, b = s.at[pl.ds(0, hi - max(lo, 1)), pl.ds(0, count)], s.at[pl.ds(0, hi - lo), pl.ds(0, count)]
        sent.append((1, lambda a=a, at=at: await_bytes(a, ssem.at[at])))
        sent.append((1, lambda b=b, at=to: await_bytes(b, ssem.at[at])))
    for k, h, ch, many, start in found:
        for b in range(log2(group_of[k] // h)):
            sent.append((1, lambda a=wx.at[b, pl.ds(start, many * ch)], at=far_at[k, b]: await_bytes(a, ssem.at[at])))

    ready(low - 1, got_v, in_v)
    for l in range(low - 1, -1, -1):
        p[l] = tdot(v[l], x[...].astype(bf))
    ready(top - 1, got_u, in_u)
    for l in range(low - 1, -1, -1):
        w3[l] = tdot(v[l], u[top - 1]).astype(bf)
    in_pair.wait_recv()
    c3 = (partial + rs3[...].astype(f32)).astype(bf)
    for l in range(low - 1, -1, -1):
        p[l] = p[l] - dot(w3[l], c3)
    g2[...] = p[low - 1].astype(bf)

    @pl.when(col == 0)
    def _():
        pl.semaphore_wait(go_node, 1)

    come_g2 = scatter(g2, gr2, group_of[low - 1])

    @pl.when(col == 1)
    def _():
        for (lo, hi, count), at, to in zip(kinds, to_s, to_other):
            await_bytes(s.at[pl.ds(0, hi - max(lo, 1)), pl.ds(0, count)], rsem.at[at])
            block = s.at[pl.ds(first_of(in_node, hi) if lo == 0 else first_of(in_node, hi) + lo - (in_node & lo), hi - lo), pl.ds(0, count)]
            push(block, block, me, to, 0)

    got_it.wait()
    out[...] = it[...].astype(f32) - x[...] + dot(u[top - 1], c3)
    @pl.when(col == 0)
    def _():
        for (lo, hi, count), to in zip(kinds, to_other):
            await_bytes(s.at[pl.ds(0, hi - lo), pl.ds(0, count)], rsem.at[to])

    if sh < most:

        @pl.when(col == 1)
        def _():
            pl.semaphore_wait(near, 1)
            signal(go_all, core=0)

        @pl.when(col == 0)
        def _():
            pl.semaphore_wait(go_all, 1)

    terms, _ = sums(n, levels, rank)
    sorts = classes_of(terms)
    term = {low - 1: g2[...]}
    for k, h, ch, many, start in reversed(found):
        for l in range(many - 1, -1, -1):
            matrix = s[pl.ds(first_of(in_node, h), h), pl.ds(start + l * ch, ch)].reshape(rank, rank)
            p[l] = p[l] - dot(matrix, term[k])
        term[k - 1] = p[k - 1].astype(bf)
        _, h, ch, _, start = terms[k - 1]
        gs[pl.ds(first_of(in_all, h), h), pl.ds(start, ch)] = term[k - 1].reshape(h, ch, vecs)
    come_g = []
    for lo, hi, count in reversed(sorts):
        part = pl.ds(0, count)
        at = slot()
        for o in range(hi - 1, max(lo, 1) - 1, -1):
            push(gs.at[in_all ^ o, part], gr.at[o, part], me ^ o, at)
        a = gr.at[pl.ds(max(lo, 1), hi - max(lo, 1)), part]
        sent.append((None, lambda a=a, at=at: await_bytes(a, ssem.at[at])))
        come_g.append(lambda a=a, at=at: await_bytes(a, rsem.at[at]))

    come_g2()
    h = min(group_of[low - 1], most)
    ch = rank // h
    share = pl.ds(pl.multiple_of((me & (h - 1)) * ch, 16), ch)
    total = total_of(
        g2[share], lambda o: gr2[pl.ds((o - 1) * ch, ch)], gx.at[low - 1], gy.at[low - 1], group_of[low - 1])
    c2[share] = total.astype(bf)
    come_c2 = gather(c2, group_of[low - 1])

    for come in come_g:
        come()
    for l, h, ch, _, start in terms:
        part = pl.ds(start, ch)
        total = total_of(gs[in_all, part], lambda o: gr[o, part], gx.at[l], gy.at[l], group_of[l])
        c[in_all, part] = total.astype(bf)
    come_c = []
    for lo, hi, count in reversed(sorts):
        part = pl.ds(0, count)
        at = slot()
        for o in range(hi - 1, max(lo, 1) - 1, -1):
            push(c.at[in_all, part], c.at[in_all, part], me ^ o, at)
        a = c.at[pl.ds(0, hi - max(lo, 1)), part]
        sent.append((None, lambda a=a, at=at: await_bytes(a, ssem.at[at])))
        come_c.append(lambda a=a, at=at: await_bytes(a, rsem.at[at]))
    ready(low - 1, got_u, in_u)
    come_c2()
    out[...] = out[...] + dot(u[low - 1], c2[...])
    for l in range(low - 2, -1, -1):
        ready(l, got_u, in_u)
    for come in come_c:
        come()
    whole = {
        l: c[pl.ds(first_of(in_all, h), h), pl.ds(start, ch)].reshape(rank, vecs) for l, h, ch, _, start in terms
    }

    num = jnp.zeros((1, vecs), f32)
    den = jnp.zeros((1, vecs), f32)
    blocks = 4
    size = rows // blocks
    for k in range(blocks):
        b = pl.ds(k * size, size)
        updated = out[b]
        for l in whole:
            updated = updated + dot(u[l, b], whole[l])
        out[b] = updated
        num = num + jnp.sum(updated * r[b].astype(f32), axis=0, keepdims=True)
        den = den + jnp.sum(updated * updated, axis=0, keepdims=True)
    st[pl.ds(0, 1)] = num
    st[pl.ds(1, 1)] = den
    at = slot()
    for o in range(most - 1, 0, -1):
        push(st, sg.at[o - 1], me ^ o, at)
    sent.append((None, lambda: await_bytes(sg, ssem.at[at])))
    got_est.wait()
    await_bytes(sg, rsem.at[at])
    total = st[...]
    for o in range(1, most):
        total = total + sg[o - 1]
    for b in range(log2(n // most)):
        sx[0, b] = total
        lone(sx.at[0, b], sx.at[1, b], me ^ (most << b)).wait_recv()
        total = total + sx[1, b]
    fun[...] = (est[...] + total[0:1] / (total[1:2] + epsilon)).reshape(vecs)
    for where, done in sent:
        if where is None:
            done()
        else:
            pl.when(col == where)(done)


def finish(updated, functional, out, fun, sem):
    copies = [
        pltpu.make_async_copy(updated, out, sem.at[0]),
        pltpu.make_async_copy(functional, fun, sem.at[1]),
    ]
    for copy in copies:
        copy.start()
    for copy in copies:
        copy.wait()


def per_device(n, iterate, residual, leaf_offset, bases_v, bases_u, estimate):
    rows, vecs = residual.shape
    levels = bases_v.shape[0]
    rank = 2 * bases_v.shape[2]
    width = 2 * leaf_offset.shape[1]
    low = levels - 2
    far = log2(n // min(n, MOST))
    slots = 2 * levels + 8 * low + far * (2 * low + 1) + 8
    found = scratch_of(n, levels, rows, rank, vecs, width)
    anywhere = pl.BlockSpec(memory_space=pl.ANY)
    vmem = pl.BlockSpec(memory_space=pltpu.VMEM)
    args = (iterate, residual, leaf_offset, bases_v, bases_u, estimate.reshape(1, vecs))
    shapes = (
        jax.ShapeDtypeStruct((rows, vecs), jnp.float32),
        jax.ShapeDtypeStruct((vecs,), jnp.float32),
    )
    results = pl.pallas_call(
        functools.partial(kernel, n, [name for name, _, _ in found]),
        out_shape=shapes,
        in_specs=[anywhere] * 6,
        out_specs=(vmem, vmem),
        scratch_shapes=[pltpu.VMEM(shape, kind) for _, kind, shape in found] + [
            pltpu.SemaphoreType.DMA((2 * levels + 2 * (rows // width) + 4,)),
            pltpu.SemaphoreType.DMA((slots,)),
            pltpu.SemaphoreType.DMA((slots,)),
        ] + [pltpu.SemaphoreType.REGULAR] * 5,
        compiler_params=pltpu.CompilerParams(
            collective_id=0, has_side_effects=True, vmem_limit_bytes=44 << 20
        ),
    )(*(pltpu.with_memory_space_constraint(a, pltpu.HBM) for a in args))
    return pl.pallas_call(
        finish,
        out_shape=shapes,
        in_specs=[vmem] * 2,
        out_specs=(anywhere, anywhere),
        scratch_shapes=[pltpu.SemaphoreType.DMA((2,))],
    )(*(pltpu.with_memory_space_constraint(a, pltpu.VMEM) for a in results))


def solution(mesh):
    return jax.shard_map(
        functools.partial(per_device, mesh.shape["rows"]),
        mesh=mesh,
        in_specs=(
            P("rows", "cols"),
            P("rows", "cols"),
            P("rows", "cols"),
            P(None, "rows", "cols"),
            P(None, "rows", "cols"),
            P("cols"),
        ),
        out_specs=(P("rows", "cols"), P("cols")),
        check_vma=False,
    )
```

```python
import functools

import jax
import jax.numpy as jnp
from jax import lax
from jax.experimental import pallas as pl
from jax.experimental.pallas import tpu as pltpu
from jax.sharding import PartitionSpec as P

epsilon = 1e-06
MESH = pl.DeviceIdType.MESH
MOST = 16
CUTS = 1


def log2(value):
    return value.bit_length() - 1


def tdot(a, b):
    return lax.dot_general(a, b, (((0,), (0,)), ((), ())), preferred_element_type=jnp.float32)


def dot(a, b):
    return jnp.dot(a, b, preferred_element_type=jnp.float32)


def shares(n, levels, rank, which, most):
    found, start = [], 0
    for level, many in which:
        h = min(2 ** (levels - 1 - level), most)
        found.append((level, h, rank // h, many, start))
        start += many * (rank // h)
    return found, start


def classes_of(found):
    out, low = [], 0
    for level, h, ch, many, start in reversed(found):
        if h > low:
            out.append((low, h, start + many * ch))
            low = h
    return out


def crosses(n, levels, rank):
    return shares(n, levels, rank, [(k, k) for k in range(1, levels - 2)], MOST)


def sums(n, levels, rank):
    return shares(n, levels, rank, [(l, 1) for l in range(levels - 3)], MOST)


def scratch_of(n, levels, rows, rank, vecs, width):
    half, top = rank // 2, levels - 1
    low = top - 1
    most = min(n, MOST)
    room = max(log2(n // most), 1)
    bf, f32 = jnp.bfloat16, jnp.float32
    sh = min(n // 2, MOST)
    _, cross_rows = crosses(n, levels, rank)
    _, sum_rows = sums(n, levels, rank)
    return [
        ("it", bf, (rows, vecs)),
        ("r", bf, (rows, vecs)),
        ("rp", bf, (rows, vecs)),
        ("leaf", bf, (rows, width)),
        ("v", bf, (levels, rows, rank)),
        ("u", bf, (levels, rows, rank)),
        ("est", f32, (1, vecs)),
        ("x", f32, (rows, vecs)),
        ("xu", bf, (rows, vecs + rank)),
        ("w3", bf, (low, rank, rank)),
        ("p", f32, (low, rank, vecs)),
        ("ps3", bf, (rank, vecs)),
        ("rs3", bf, (rank, vecs)),
        ("g2", bf, (rank, vecs)),
        ("gr2", bf, (rank, vecs)),
        ("c2", bf, (rank, vecs)),
        ("gs", bf, (most, sum_rows, vecs)),
        ("gr", bf, (2, most, sum_rows, vecs)),
        ("c", bf, (most, sum_rows, vecs)),
        ("c0", bf, (sum_rows, vecs)),
        ("gx", f32, (low, room, 2, rank // most, vecs)),
        ("gy", f32, (low, room, 2, rank // most, vecs)),
        ("ws", bf, (sh, cross_rows, half)),
        ("wr", bf, (2, sh, cross_rows, half)),
        ("s", bf, (sh, cross_rows, rank)),
        ("wx", f32, (room, cross_rows, rank)),
        ("wy", f32, (room, cross_rows, rank)),
        ("st", f32, (2, vecs)),
        ("sg", f32, (most - 1, 2, vecs)),
        ("sx", f32, (2, room, 2, vecs)),
    ]


def kernel(n, names, it_h, r_h, leaf_h, v_h, u_h, est_h, out, fun, *refs):
    buf = dict(zip(names, refs))
    lsem, ssem, rsem, hs, go, go_node, near, go_all = refs[len(names):]
    it, r, rp, leaf, v, u, est, x, xu = (buf[a] for a in ("it", "r", "rp", "leaf", "v", "u", "est", "x", "xu"))
    w3, p, ps3, rs3, g2, gr2, c2 = (buf[a] for a in ("w3", "p", "ps3", "rs3", "g2", "gr2", "c2"))
    gs, gr, c, c0, gx, gy, ws, wr, s, wx, wy = (
        buf[a] for a in ("gs", "gr", "c", "c0", "gx", "gy", "ws", "wr", "s", "wx", "wy"))
    st, sg, sx = (buf[a] for a in ("st", "sg", "sx"))
    bf, f32 = jnp.bfloat16, jnp.float32
    rows, vecs = r.shape
    levels, _, rank = v.shape
    half = rank // 2
    width = leaf.shape[1]
    lh = width // 2
    leaves = rows // width
    top = levels - 1
    low = top - 1
    most = min(n, MOST)
    sh = min(n // 2, MOST)
    me = lax.axis_index("rows")
    col = lax.axis_index("cols")
    other = 1 - col
    mine = pl.ds(pl.multiple_of(col * half, half), half)
    beside = pl.ds(pl.multiple_of(vecs + col * half, half), half)
    in_node = me & (sh - 1)
    in_all = me & (most - 1)
    group_of = [2 ** (top - l) for l in range(levels)]

    def signal(sem, to=None, core=None):
        device = {} if to is None else {"rows": to}
        if core is not None:
            device["cols"] = core
        pl.semaphore_signal(sem, inc=1, device_id=device, device_id_type=MESH)

    barrier = pltpu.get_barrier_semaphore()
    partners = [1] + [1 << b for b in range(log2(sh), log2(n))]

    @pl.when(col == 1)
    def _():
        signal(barrier, core=0)
        for o in range(sh - 1, 1, -1):
            signal(barrier, me ^ o)

    used = {"l": 0, "s": 0}

    def fetch(src, dst):
        copy = pltpu.make_async_copy(src, dst, lsem.at[used["l"]])
        used["l"] += 1
        copy.start()
        return copy

    got_v, got_u = {}, {}

    def fetch_v(l):
        got_v[l] = fetch(v_h.at[l], v.at[l, :, mine])

    def fetch_u(l):
        got_u[l] = fetch(u_h.at[l], xu.at[:, beside] if l == top - 1 else u.at[l, :, mine])

    for l in range(low - 1):
        fetch_v(l)
        fetch_u(l + 1)

    @pl.when(col == 0)
    def _():
        pl.semaphore_wait(barrier, 1)
        signal(hs, core=1)

    @pl.when(col == 1)
    def _():
        pl.semaphore_wait(hs, 1)
        for o in partners:
            signal(barrier, me ^ o)

    sent = []

    def await_bytes(ref, sem):
        pltpu.make_async_copy(ref, ref, sem).wait()

    def slot(many=1):
        used["s"] += many
        return used["s"] - many

    def push(src, dst, to=None, at=None, core=None):
        at = slot() if at is None else at
        device = {} if to is None else {"rows": to}
        if to is None or core is not None:
            device["cols"] = other if core is None else core
        copy = pltpu.make_async_remote_copy(
            src_ref=src, dst_ref=dst, send_sem=ssem.at[at], recv_sem=rsem.at[at],
            device_id=device, device_id_type=MESH)
        copy.start()
        return copy

    def lone(src, dst, to=None):
        copy = push(src, dst, to)
        sent.append((None, copy.wait_send))
        return copy

    in_v, in_u = {}, {}

    def push_v(l):
        in_v[l] = lone(v_h.at[l], v.at[l, :, mine])

    def push_u(l):
        in_u[l] = lone(u_h.at[l], xu.at[:, beside] if l == top - 1 else u.at[l, :, mine])

    for l in range(low - 1):
        push_v(l)
    got_r = [fetch(r_h, r)]
    for k in range(leaves):
        for part, which in enumerate((col, other)):
            start = pl.multiple_of(k * width + which * lh, 16)
            got_r.append(fetch(r_h.at[pl.ds(start, lh)], rp.at[pl.ds(k * width + part * lh, lh)]))
    got_leaf = fetch(leaf_h, leaf.at[:, pl.ds(0, lh)])
    in_leaf = lone(leaf_h, leaf.at[:, pl.ds(lh, lh)])
    for l in (top, top - 1):
        fetch_v(l)
        push_v(l)
        fetch_u(l)
        push_u(l)
    fetch_v(low - 1)
    push_v(low - 1)
    fetch_u(0)
    for l in range(low - 1, -1, -1):
        push_u(l)
    got_it = fetch(it_h, it)
    got_est = fetch(est_h, est)

    def ready(l, got, come):
        if l in got:
            got.pop(l).wait()
        come[l].wait_recv()

    def scatter(src, dst, group):
        h = min(group, most)
        ch = rank // h
        j = me & (h - 1)
        at = slot()
        for o in range(h - 1, 0, -1):
            push(src.at[pl.ds(pl.multiple_of((j ^ o) * ch, 16), ch)], dst.at[pl.ds((o - 1) * ch, ch)], me ^ o, at)
        whole = dst.at[pl.ds(0, (h - 1) * ch)]
        sent.append((None, lambda: await_bytes(whole, ssem.at[at])))
        return lambda: await_bytes(whole, rsem.at[at])

    def gather(ref, group):
        h = min(group, most)
        ch = rank // h
        share = pl.ds(pl.multiple_of((me & (h - 1)) * ch, 16), ch)
        at = slot()
        for o in range(h - 1, 0, -1):
            push(ref.at[share], ref.at[share], me ^ o, at)
        whole = ref.at[pl.ds(0, (h - 1) * ch)]
        sent.append((None, lambda: await_bytes(whole, ssem.at[at])))
        return lambda: await_bytes(whole, rsem.at[at])

    def first_of(j, h):
        return j - (j & (h - 1))

    for copy in got_r:
        copy.wait()
    got_leaf.wait()
    for k in range(leaves):
        b = pl.ds(k * width, width)
        x[b] = r[b].astype(f32) + dot(leaf[b, pl.ds(0, lh)], rp[pl.ds(k * width, lh)])

    found, _ = crosses(n, levels, rank)
    kinds = classes_of(found)
    for k in range(1, low):
        got_u.pop(k).wait()
    for l in range(low - 1):
        ready(l, got_v, in_v)
        below = jnp.concatenate([u[k, :, mine] for k in range(l + 1, low)], axis=1)
        product = tdot(v[l], below).astype(bf)
        for i, (k, h, ch, _, start) in enumerate(found[l:]):
            ws[pl.ds(first_of(in_node, h), h), pl.ds(start + l * ch, ch)] = (
                product[:, i * half:(i + 1) * half].reshape(h, ch, half))

    @pl.when(col == 1)
    def _():
        pl.semaphore_wait(barrier, sh - 2 + len(partners))
        signal(go, core=0)

    @pl.when(col == 0)
    def _():
        pl.semaphore_wait(go, 1)

    to_w = [slot(2) for _ in kinds]
    to_s = [slot() for _ in kinds]
    to_other = [slot() for _ in kinds]
    for (lo, hi, count), at in reversed(list(zip(kinds, to_w))):
        part = pl.ds(0, count)
        for o in range(hi - 1, max(lo, 1) - 1, -1):
            push(ws.at[in_node ^ o, part], wr.at[col, o, part], me ^ o, at + col, 1)
        if lo == 0:

            @pl.when(col == 0)
            def _():
                push(ws.at[in_node, part], wr.at[0, 0, part], me, at, 1)

        a, b = ws.at[pl.ds(0, hi - lo), part], ws.at[pl.ds(0, hi - max(lo, 1)), part]
        sent.append((0, lambda a=a, at=at: await_bytes(a, ssem.at[at])))
        sent.append((1, lambda b=b, at=at: await_bytes(b, ssem.at[at + 1])))

    in_leaf.wait_recv()
    for k in range(leaves):
        b = pl.ds(k * width, width)
        x[b] = x[b] + dot(leaf[b, pl.ds(lh, lh)], rp[pl.ds(k * width + lh, lh)])
    ready(top, got_v, in_v)
    narrow = tdot(v[top], x[...].astype(bf)).astype(bf)
    ready(top, got_u, in_u)
    x[...] = x[...] - dot(u[top], narrow)
    xu[:, pl.ds(0, vecs)] = x[...].astype(bf)
    ready(top - 1, got_v, in_v)
    partial = tdot(v[top - 1], xu[:, pl.ds(0, vecs)])
    ps3[...] = partial.astype(bf)
    in_pair = lone(ps3, rs3, me ^ 1)

    far_at = {(k, b): slot() for k, h, _, _, _ in found for b in range(log2(group_of[k] // h))}

    @pl.when(col == 1)
    def _():
        for (lo, hi, count), at in zip(kinds, to_w):
            await_bytes(wr.at[0, pl.ds(lo, hi - lo), pl.ds(0, count)], rsem.at[at])
            await_bytes(wr.at[1, pl.ds(max(lo, 1), hi - max(lo, 1)), pl.ds(0, count)], rsem.at[at + 1])
        for k, h, ch, many, start in found:
            part = pl.ds(start, many * ch)
            first, second = wr[0, 0, part].astype(f32), ws[in_node, part].astype(f32)
            for o in range(1, h):
                first = first + wr[0, o, part].astype(f32)
                second = second + wr[1, o, part].astype(f32)
            for b in range(log2(group_of[k] // h)):
                wx[b, part, pl.ds(0, half)] = first
                wx[b, part, pl.ds(half, half)] = second
                push(wx.at[b, part], wy.at[b, part], me ^ (most << b), far_at[k, b]).wait_recv()
                first = first + wy[b, part, pl.ds(0, half)]
                second = second + wy[b, part, pl.ds(half, half)]
            s[in_node, part, pl.ds(0, half)] = first.astype(bf)
            s[in_node, part, pl.ds(half, half)] = second.astype(bf)
        for (lo, hi, count), at in reversed(list(zip(kinds, to_s))):
            share = s.at[in_node, pl.ds(0, count)]
            for o in range(hi - 1, max(lo, 1) - 1, -1):
                push(share, share, me ^ o, at)
        signal(go_node, core=0)
        if sh < most:
            signal(near, me ^ sh)

    for (lo, hi, count), at, to in zip(kinds, to_s, to_other):
        a, b = s.at[pl.ds(0, hi - max(lo, 1)), pl.ds(0, count)], s.at[pl.ds(0, hi - lo), pl.ds(0, count)]
        sent.append((1, lambda a=a, at=at: await_bytes(a, ssem.at[at])))
        sent.append((1, lambda b=b, at=to: await_bytes(b, ssem.at[at])))
    for k, h, ch, many, start in found:
        for b in range(log2(group_of[k] // h)):
            sent.append((1, lambda a=wx.at[b, pl.ds(start, many * ch)], at=far_at[k, b]: await_bytes(a, ssem.at[at])))

    ready(low - 1, got_v, in_v)
    ready(top - 1, got_u, in_u)
    for l in range(low - 1, -1, -1):
        product = tdot(v[l], xu[...])
        p[l] = product[:, :vecs]
        w3[l] = product[:, vecs:].astype(bf)
    in_pair.wait_recv()
    c3 = (partial + rs3[...].astype(f32)).astype(bf)
    p[...] = p[...] - dot(w3[...].reshape(low * rank, rank), c3).reshape(low, rank, vecs)
    g2[...] = p[low - 1].astype(bf)

    @pl.when(col == 0)
    def _():
        pl.semaphore_wait(go_node, 1)

    come_g2 = scatter(g2, gr2, group_of[low - 1])

    @pl.when(col == 1)
    def _():
        for (lo, hi, count), at, to in zip(kinds, to_s, to_other):
            await_bytes(s.at[pl.ds(0, hi - max(lo, 1)), pl.ds(0, count)], rsem.at[at])
            block = s.at[pl.ds(first_of(in_node, hi) if lo == 0 else first_of(in_node, hi) + lo - (in_node & lo), hi - lo), pl.ds(0, count)]
            push(block, block, me, to, 0)

    @pl.when(col == 0)
    def _():
        for (lo, hi, count), to in zip(kinds, to_other):
            await_bytes(s.at[pl.ds(0, hi - lo), pl.ds(0, count)], rsem.at[to])

    if sh < most:

        @pl.when(col == 1)
        def _():
            pl.semaphore_wait(near, 1)
            signal(go_all, core=0)

        @pl.when(col == 0)
        def _():
            pl.semaphore_wait(go_all, 1)

    terms, _ = sums(n, levels, rank)
    sorts = classes_of(terms)
    term = {low - 1: g2[...]}
    for k, h, ch, many, start in reversed(found):
        for l in range(many - 1, -1, -1):
            matrix = s[pl.ds(first_of(in_node, h), h), pl.ds(start + l * ch, ch)].reshape(rank, rank)
            p[l] = p[l] - dot(matrix, term[k])
        term[k - 1] = p[k - 1].astype(bf)
        _, h, ch, _, start = terms[k - 1]
        gs[pl.ds(first_of(in_all, h), h), pl.ds(start, ch)] = term[k - 1].reshape(h, ch, vecs)
    to_g = [slot(2) for _ in sorts]
    to_c = [slot(2) for _ in sorts]
    far_g = {(l, b): slot(2) for l, h, _, _, _ in terms for b in range(log2(group_of[l] // h))}
    for (lo, hi, count), at in reversed(list(zip(sorts, to_g))):
        part = pl.ds(0, count)
        for o in range(hi - 1, max(lo, 1) - 1, -1):
            push(gs.at[in_all ^ o, part], gr.at[col, o, part], me ^ o, at + col, 1)
        if lo == 0:

            @pl.when(col == 0)
            def _():
                push(gs.at[in_all, part], gr.at[0, 0, part], me, at, 1)

        a, b = gs.at[pl.ds(0, hi - lo), part], gs.at[pl.ds(0, hi - max(lo, 1)), part]
        sent.append((0, lambda a=a, at=at: await_bytes(a, ssem.at[at])))
        sent.append((1, lambda b=b, at=at: await_bytes(b, ssem.at[at + 1])))

    got_it.wait()
    out[...] = it[...].astype(f32) - x[...] + dot(xu[:, pl.ds(vecs, rank)], c3)
    come_g2()
    h = min(group_of[low - 1], most)
    ch = rank // h
    share = pl.ds(pl.multiple_of((me & (h - 1)) * ch, 16), ch)
    total = g2[share].astype(f32)
    for o in range(1, h):
        total = total + gr2[pl.ds((o - 1) * ch, ch)].astype(f32)
    c2[share] = total.astype(bf)
    come_c2 = gather(c2, group_of[low - 1])

    @pl.when(col == 1)
    def _():
        for which in (1, 0):
            for (lo, hi, count), at in zip(sorts, to_g):
                begin = max(lo, which)
                await_bytes(gr.at[which, pl.ds(begin, hi - begin), pl.ds(0, count)], rsem.at[at + which])
            for l, h, ch, _, start in terms:
                part = pl.ds(start, ch)
                total = (gs[in_all, part] if which else gr[0, 0, part]).astype(f32)
                for o in range(1, h):
                    total = total + gr[which, o, part].astype(f32)
                for b in range(log2(group_of[l] // h)):
                    gx[l, b, which] = total
                    push(gx.at[l, b, which], gy.at[l, b, which], me ^ (most << b), far_g[l, b] + which).wait_recv()
                    total = total + gy[l, b, which]
                if which:
                    c[in_all, part] = total.astype(bf)
                else:
                    c0[part] = total.astype(bf)
            for (lo, hi, count), at in reversed(list(zip(sorts, to_c))):
                part = pl.ds(0, count)
                share = c.at[in_all, part] if which else c0.at[part]
                for o in range(hi - 1, max(lo, which) - 1, -1):
                    push(share, c.at[in_all, part], me ^ o, at + which, which)

    for l, b in far_g:
        for which in range(2):
            sent.append((1, lambda a=gx.at[l, b, which], at=far_g[l, b] + which: await_bytes(a, ssem.at[at])))
    for (lo, hi, count), at in zip(sorts, to_c):
        a, b = c.at[pl.ds(0, hi - lo), pl.ds(0, count)], c.at[pl.ds(0, hi - max(lo, 1)), pl.ds(0, count)]
        sent.append((1, lambda a=a, at=at: await_bytes(a, ssem.at[at])))
        sent.append((1, lambda b=b, at=at: await_bytes(b, ssem.at[at + 1])))
    ready(low - 1, got_u, in_u)
    come_c2()
    out[...] = out[...] + dot(u[low - 1], c2[...])
    for l in range(low - 2, -1, -1):
        ready(l, got_u, in_u)
    for (lo, hi, count), at in zip(sorts, to_c):
        a, b = c.at[pl.ds(0, hi - lo), pl.ds(0, count)], c.at[pl.ds(0, hi - max(lo, 1)), pl.ds(0, count)]

        @pl.when(col == 0)
        def _():
            await_bytes(a, rsem.at[at])

        @pl.when(col == 1)
        def _():
            await_bytes(b, rsem.at[at + 1])

    whole = jnp.concatenate(
        [c[pl.ds(first_of(in_all, h), h), pl.ds(start, ch)].reshape(rank, vecs) for l, h, ch, _, start in terms])

    num = jnp.zeros((1, vecs), f32)
    den = jnp.zeros((1, vecs), f32)
    blocks = 4
    size = rows // blocks
    for k in range(blocks):
        b = pl.ds(k * size, size)
        updated = out[b] + dot(jnp.concatenate([u[l, b] for l, _, _, _, _ in terms], axis=1), whole)
        out[b] = updated
        num = num + jnp.sum(updated * r[b].astype(f32), axis=0, keepdims=True)
        den = den + jnp.sum(updated * updated, axis=0, keepdims=True)
    st[pl.ds(0, 1)] = num
    st[pl.ds(1, 1)] = den
    at = slot()
    for o in range(most - 1, 0, -1):
        push(st, sg.at[o - 1], me ^ o, at)
    sent.append((None, lambda: await_bytes(sg, ssem.at[at])))
    got_est.wait()
    await_bytes(sg, rsem.at[at])
    total = st[...]
    for o in range(1, most):
        total = total + sg[o - 1]
    for b in range(log2(n // most)):
        sx[0, b] = total
        lone(sx.at[0, b], sx.at[1, b], me ^ (most << b)).wait_recv()
        total = total + sx[1, b]
    fun[...] = (est[...] + total[0:1] / (total[1:2] + epsilon)).reshape(vecs)
    for where, done in sent:
        if where is None:
            done()
        else:
            pl.when(col == where)(done)


def finish(updated, functional, out, fun, sem):
    size = updated.shape[0] // CUTS
    copies = [
        pltpu.make_async_copy(updated.at[pl.ds(k * size, size)], out.at[pl.ds(k * size, size)], sem.at[k])
        for k in range(CUTS)
    ] + [pltpu.make_async_copy(functional, fun, sem.at[CUTS])]
    for copy in copies:
        copy.start()
    for copy in copies:
        copy.wait()


def per_device(n, iterate, residual, leaf_offset, bases_v, bases_u, estimate):
    rows, vecs = residual.shape
    levels = bases_v.shape[0]
    rank = 2 * bases_v.shape[2]
    width = 2 * leaf_offset.shape[1]
    low = levels - 2
    far = log2(n // min(n, MOST))
    slots = 2 * levels + 10 * low + far * (3 * low + 1) + 8
    found = scratch_of(n, levels, rows, rank, vecs, width)
    anywhere = pl.BlockSpec(memory_space=pl.ANY)
    vmem = pl.BlockSpec(memory_space=pltpu.VMEM)
    args = (iterate, residual, leaf_offset, bases_v, bases_u, estimate.reshape(1, vecs))
    shapes = (
        jax.ShapeDtypeStruct((rows, vecs), jnp.float32),
        jax.ShapeDtypeStruct((vecs,), jnp.float32),
    )
    results = pl.pallas_call(
        functools.partial(kernel, n, [name for name, _, _ in found]),
        out_shape=shapes,
        in_specs=[anywhere] * 6,
        out_specs=(vmem, vmem),
        scratch_shapes=[pltpu.VMEM(shape, kind) for _, kind, shape in found] + [
            pltpu.SemaphoreType.DMA((2 * levels + 2 * (rows // width) + 4,)),
            pltpu.SemaphoreType.DMA((slots,)),
            pltpu.SemaphoreType.DMA((slots,)),
        ] + [pltpu.SemaphoreType.REGULAR] * 5,
        compiler_params=pltpu.CompilerParams(
            collective_id=0, has_side_effects=True, vmem_limit_bytes=44 << 20
        ),
    )(*(pltpu.with_memory_space_constraint(a, pltpu.HBM) for a in args))
    return pl.pallas_call(
        finish,
        out_shape=shapes,
        in_specs=[vmem] * 2,
        out_specs=(anywhere, anywhere),
        scratch_shapes=[pltpu.SemaphoreType.DMA((CUTS + 1,))],
    )(*(pltpu.with_memory_space_constraint(a, pltpu.VMEM) for a in results))


def solution(mesh):
    return jax.shard_map(
        functools.partial(per_device, mesh.shape["rows"]),
        mesh=mesh,
        in_specs=(
            P("rows", "cols"),
            P("rows", "cols"),
            P("rows", "cols"),
            P(None, "rows", "cols"),
            P(None, "rows", "cols"),
            P("cols"),
        ),
        out_specs=(P("rows", "cols"), P("cols")),
        check_vma=False,
    )
```

```python
import functools

import jax
import jax.numpy as jnp
from jax import lax
from jax.experimental import pallas as pl
from jax.experimental.pallas import tpu as pltpu
from jax.sharding import PartitionSpec as P

epsilon = 1e-06
MESH = pl.DeviceIdType.MESH
MOST = 16
CUTS = 1


def log2(value):
    return value.bit_length() - 1


def tdot(a, b):
    return lax.dot_general(a, b, (((0,), (0,)), ((), ())), preferred_element_type=jnp.float32)


def dot(a, b):
    return jnp.dot(a, b, preferred_element_type=jnp.float32)


def shares(n, levels, rank, which, most):
    found, start = [], 0
    for level, many in which:
        h = min(2 ** (levels - 1 - level), most)
        found.append((level, h, rank // h, many, start))
        start += many * (rank // h)
    return found, start


def classes_of(found):
    out, low = [], 0
    for level, h, ch, many, start in reversed(found):
        if h > low:
            out.append((low, h, start + many * ch))
            low = h
    return out


def crosses(n, levels, rank):
    return shares(n, levels, rank, [(k, k) for k in range(1, levels - 2)], MOST)


def sums(n, levels, rank):
    return shares(n, levels, rank, [(l, 1) for l in range(levels - 3)], MOST)


def scratch_of(n, levels, rows, rank, vecs, width):
    half, top = rank // 2, levels - 1
    low = top - 1
    most = min(n, MOST)
    room = max(log2(n // most), 1)
    bf, f32 = jnp.bfloat16, jnp.float32
    sh = min(n // 2, MOST)
    _, cross_rows = crosses(n, levels, rank)
    _, sum_rows = sums(n, levels, rank)
    return [
        ("it", bf, (rows, vecs)),
        ("r", bf, (rows, vecs)),
        ("rp", bf, (rows, vecs)),
        ("leaf", bf, (rows, width)),
        ("v", bf, (levels, rows, rank)),
        ("u", bf, (levels, rows, rank)),
        ("est", f32, (1, vecs)),
        ("x", f32, (rows, vecs)),
        ("xu", bf, (rows, vecs + rank)),
        ("w3", bf, (low, rank, rank)),
        ("p", f32, (low, rank, vecs)),
        ("ps3", bf, (rank, vecs)),
        ("rs3", bf, (rank, vecs)),
        ("g2", bf, (rank, vecs)),
        ("gr2", bf, (rank, vecs)),
        ("c2", bf, (rank, vecs)),
        ("gs", bf, (most, sum_rows, vecs)),
        ("gr", bf, (2, most, sum_rows, vecs)),
        ("c", bf, (most, sum_rows, vecs)),
        ("c0", bf, (sum_rows, vecs)),
        ("gx", f32, (low, room, 2, rank // most, vecs)),
        ("gy", f32, (low, room, 2, rank // most, vecs)),
        ("ws", bf, (sh, cross_rows, half)),
        ("wr", bf, (2, sh, cross_rows, half)),
        ("s", bf, (sh, cross_rows, rank)),
        ("wx", f32, (room, cross_rows, rank)),
        ("wy", f32, (room, cross_rows, rank)),
        ("st", f32, (2, vecs)),
        ("sg", f32, (most - 1, 2, vecs)),
        ("sx", f32, (2, room, 2, vecs)),
    ]


def kernel(n, names, it_h, r_h, leaf_h, v_h, u_h, est_h, out, fun, *refs):
    buf = dict(zip(names, refs))
    lsem, ssem, rsem, hs, go, go_node, near, go_all = refs[len(names):]
    it, r, rp, leaf, v, u, est, x, xu = (buf[a] for a in ("it", "r", "rp", "leaf", "v", "u", "est", "x", "xu"))
    w3, p, ps3, rs3, g2, gr2, c2 = (buf[a] for a in ("w3", "p", "ps3", "rs3", "g2", "gr2", "c2"))
    gs, gr, c, c0, gx, gy, ws, wr, s, wx, wy = (
        buf[a] for a in ("gs", "gr", "c", "c0", "gx", "gy", "ws", "wr", "s", "wx", "wy"))
    st, sg, sx = (buf[a] for a in ("st", "sg", "sx"))
    bf, f32 = jnp.bfloat16, jnp.float32
    rows, vecs = r.shape
    levels, _, rank = v.shape
    half = rank // 2
    width = leaf.shape[1]
    lh = width // 2
    leaves = rows // width
    top = levels - 1
    low = top - 1
    most = min(n, MOST)
    sh = min(n // 2, MOST)
    me = lax.axis_index("rows")
    col = lax.axis_index("cols")
    other = 1 - col
    mine = pl.ds(pl.multiple_of(col * half, half), half)
    beside = pl.ds(pl.multiple_of(vecs + col * half, half), half)
    in_node = me & (sh - 1)
    in_all = me & (most - 1)
    group_of = [2 ** (top - l) for l in range(levels)]

    def signal(sem, to=None, core=None):
        device = {} if to is None else {"rows": to}
        if core is not None:
            device["cols"] = core
        pl.semaphore_signal(sem, inc=1, device_id=device, device_id_type=MESH)

    barrier = pltpu.get_barrier_semaphore()
    partners = [1] + [1 << b for b in range(log2(sh), log2(n))]

    @pl.when(col == 1)
    def _():
        signal(barrier, core=0)
        for o in range(sh - 1, 1, -1):
            signal(barrier, me ^ o)

    used = {"l": 0, "s": 0}

    def fetch(src, dst):
        copy = pltpu.make_async_copy(src, dst, lsem.at[used["l"]])
        used["l"] += 1
        copy.start()
        return copy

    got_v, got_u = {}, {}

    def fetch_v(l):
        got_v[l] = fetch(v_h.at[l], v.at[l, :, mine])

    def fetch_u(l):
        got_u[l] = fetch(u_h.at[l], xu.at[:, beside] if l == top - 1 else u.at[l, :, mine])


    @pl.when(col == 0)
    def _():
        pl.semaphore_wait(barrier, 1)
        signal(hs, core=1)

    @pl.when(col == 1)
    def _():
        pl.semaphore_wait(hs, 1)
        for o in partners:
            signal(barrier, me ^ o)

    sent = []

    def drain():
        for where, done in sent:
            if where is None:
                done()
            else:
                pl.when(col == where)(done)
        sent.clear()

    def await_bytes(ref, sem):
        pltpu.make_async_copy(ref, ref, sem).wait()

    def slot(many=1):
        used["s"] += many
        return used["s"] - many

    def push(src, dst, to=None, at=None, core=None):
        at = slot() if at is None else at
        device = {} if to is None else {"rows": to}
        if to is None or core is not None:
            device["cols"] = other if core is None else core
        copy = pltpu.make_async_remote_copy(
            src_ref=src, dst_ref=dst, send_sem=ssem.at[at], recv_sem=rsem.at[at],
            device_id=device, device_id_type=MESH)
        copy.start()
        return copy

    def lone(src, dst, to=None):
        copy = push(src, dst, to)
        sent.append((None, copy.wait_send))
        return copy

    in_v, in_u = {}, {}

    def push_v(l):
        in_v[l] = lone(v_h.at[l], v.at[l, :, mine])

    def push_u(l):
        in_u[l] = lone(u_h.at[l], xu.at[:, beside] if l == top - 1 else u.at[l, :, mine])

    for l in range(low - 1):
        push_v(l)
    for l in range(low - 1):
        fetch_v(l)
        fetch_u(l + 1)
    in_leaf = lone(leaf_h, leaf.at[:, pl.ds(lh, lh)])
    got_r = [fetch(r_h, r)]
    for k in range(leaves):
        for part, which in enumerate((col, other)):
            start = pl.multiple_of(k * width + which * lh, 16)
            got_r.append(fetch(r_h.at[pl.ds(start, lh)], rp.at[pl.ds(k * width + part * lh, lh)]))
    got_leaf = fetch(leaf_h, leaf.at[:, pl.ds(0, lh)])
    for l in (top, top - 1):
        fetch_v(l)
        push_v(l)
        fetch_u(l)
        push_u(l)
    fetch_v(low - 1)
    push_v(low - 1)
    fetch_u(0)
    for l in range(low - 1, -1, -1):
        push_u(l)
    got_it = fetch(it_h, it)
    got_est = fetch(est_h, est)

    def ready(l, got, come):
        if l in got:
            got.pop(l).wait()
        come[l].wait_recv()

    def scatter(src, dst, group):
        h = min(group, most)
        ch = rank // h
        j = me & (h - 1)
        at = slot()
        for o in range(h - 1, 0, -1):
            push(src.at[pl.ds(pl.multiple_of((j ^ o) * ch, 16), ch)], dst.at[pl.ds((o - 1) * ch, ch)], me ^ o, at)
        whole = dst.at[pl.ds(0, (h - 1) * ch)]
        sent.append((None, lambda: await_bytes(whole, ssem.at[at])))
        return lambda: await_bytes(whole, rsem.at[at])

    def gather(ref, group):
        h = min(group, most)
        ch = rank // h
        share = pl.ds(pl.multiple_of((me & (h - 1)) * ch, 16), ch)
        at = slot()
        for o in range(h - 1, 0, -1):
            push(ref.at[share], ref.at[share], me ^ o, at)
        whole = ref.at[pl.ds(0, (h - 1) * ch)]
        sent.append((None, lambda: await_bytes(whole, ssem.at[at])))
        return lambda: await_bytes(whole, rsem.at[at])

    def first_of(j, h):
        return j - (j & (h - 1))

    found, _ = crosses(n, levels, rank)
    kinds = classes_of(found)
    for k in range(1, low):
        got_u.pop(k).wait()
    for l in range(low - 1):
        ready(l, got_v, in_v)
        below = jnp.concatenate([u[k, :, mine] for k in range(l + 1, low)], axis=1)
        product = tdot(v[l], below).astype(bf)
        for i, (k, h, ch, _, start) in enumerate(found[l:]):
            ws[pl.ds(first_of(in_node, h), h), pl.ds(start + l * ch, ch)] = (
                product[:, i * half:(i + 1) * half].reshape(h, ch, half))

    @pl.when(col == 1)
    def _():
        pl.semaphore_wait(barrier, sh - 2 + len(partners))
        signal(go, core=0)

    @pl.when(col == 0)
    def _():
        pl.semaphore_wait(go, 1)

    to_w = [slot(2) for _ in kinds]
    to_s = [slot() for _ in kinds]
    to_other = [slot() for _ in kinds]
    for (lo, hi, count), at in reversed(list(zip(kinds, to_w))):
        part = pl.ds(0, count)
        for o in range(hi - 1, max(lo, 1) - 1, -1):
            push(ws.at[in_node ^ o, part], wr.at[col, o, part], me ^ o, at + col, 1)
        if lo == 0:

            @pl.when(col == 0)
            def _():
                push(ws.at[in_node, part], wr.at[0, 0, part], me, at, 1)

        a, b = ws.at[pl.ds(0, hi - lo), part], ws.at[pl.ds(0, hi - max(lo, 1)), part]
        sent.append((0, lambda a=a, at=at: await_bytes(a, ssem.at[at])))
        sent.append((1, lambda b=b, at=at: await_bytes(b, ssem.at[at + 1])))

    for copy in got_r:
        copy.wait()
    got_leaf.wait()
    for k in range(leaves):
        b = pl.ds(k * width, width)
        x[b] = r[b].astype(f32) + dot(leaf[b, pl.ds(0, lh)], rp[pl.ds(k * width, lh)])

    in_leaf.wait_recv()
    for k in range(leaves):
        b = pl.ds(k * width, width)
        x[b] = x[b] + dot(leaf[b, pl.ds(lh, lh)], rp[pl.ds(k * width + lh, lh)])
    ready(top, got_v, in_v)
    narrow = tdot(v[top], x[...].astype(bf)).astype(bf)
    ready(top, got_u, in_u)
    x[...] = x[...] - dot(u[top], narrow)
    xu[:, pl.ds(0, vecs)] = x[...].astype(bf)
    ready(top - 1, got_v, in_v)
    partial = tdot(v[top - 1], xu[:, pl.ds(0, vecs)])
    ps3[...] = partial.astype(bf)
    in_pair = lone(ps3, rs3, me ^ 1)

    far_at = {(k, b): slot() for k, h, _, _, _ in found for b in range(log2(group_of[k] // h))}

    @pl.when(col == 1)
    def _():
        for (lo, hi, count), at in zip(kinds, to_w):
            await_bytes(wr.at[0, pl.ds(lo, hi - lo), pl.ds(0, count)], rsem.at[at])
            await_bytes(wr.at[1, pl.ds(max(lo, 1), hi - max(lo, 1)), pl.ds(0, count)], rsem.at[at + 1])
        for k, h, ch, many, start in found:
            part = pl.ds(start, many * ch)
            first, second = wr[0, 0, part].astype(f32), ws[in_node, part].astype(f32)
            for o in range(1, h):
                first = first + wr[0, o, part].astype(f32)
                second = second + wr[1, o, part].astype(f32)
            for b in range(log2(group_of[k] // h)):
                wx[b, part, pl.ds(0, half)] = first
                wx[b, part, pl.ds(half, half)] = second
                push(wx.at[b, part], wy.at[b, part], me ^ (most << b), far_at[k, b]).wait_recv()
                first = first + wy[b, part, pl.ds(0, half)]
                second = second + wy[b, part, pl.ds(half, half)]
            s[in_node, part, pl.ds(0, half)] = first.astype(bf)
            s[in_node, part, pl.ds(half, half)] = second.astype(bf)
        for (lo, hi, count), at in reversed(list(zip(kinds, to_s))):
            share = s.at[in_node, pl.ds(0, count)]
            for o in range(hi - 1, max(lo, 1) - 1, -1):
                push(share, share, me ^ o, at)
        signal(go_node, core=0)
        if sh < most:
            signal(near, me ^ sh)

    for (lo, hi, count), at, to in zip(kinds, to_s, to_other):
        a, b = s.at[pl.ds(0, hi - max(lo, 1)), pl.ds(0, count)], s.at[pl.ds(0, hi - lo), pl.ds(0, count)]
        sent.append((1, lambda a=a, at=at: await_bytes(a, ssem.at[at])))
        sent.append((1, lambda b=b, at=to: await_bytes(b, ssem.at[at])))
    for k, h, ch, many, start in found:
        for b in range(log2(group_of[k] // h)):
            sent.append((1, lambda a=wx.at[b, pl.ds(start, many * ch)], at=far_at[k, b]: await_bytes(a, ssem.at[at])))

    ready(low - 1, got_v, in_v)
    ready(top - 1, got_u, in_u)
    for l in range(low - 1, -1, -1):
        product = tdot(v[l], xu[...])
        p[l] = product[:, :vecs]
        w3[l] = product[:, vecs:].astype(bf)
    in_pair.wait_recv()
    c3 = (partial + rs3[...].astype(f32)).astype(bf)
    p[...] = p[...] - dot(w3[...].reshape(low * rank, rank), c3).reshape(low, rank, vecs)
    g2[...] = p[low - 1].astype(bf)

    @pl.when(col == 0)
    def _():
        pl.semaphore_wait(go_node, 1)

    come_g2 = scatter(g2, gr2, group_of[low - 1])

    @pl.when(col == 1)
    def _():
        for (lo, hi, count), at, to in zip(kinds, to_s, to_other):
            await_bytes(s.at[pl.ds(0, hi - max(lo, 1)), pl.ds(0, count)], rsem.at[at])
            block = s.at[pl.ds(first_of(in_node, hi) if lo == 0 else first_of(in_node, hi) + lo - (in_node & lo), hi - lo), pl.ds(0, count)]
            push(block, block, me, to, 0)

    @pl.when(col == 0)
    def _():
        for (lo, hi, count), to in zip(kinds, to_other):
            await_bytes(s.at[pl.ds(0, hi - lo), pl.ds(0, count)], rsem.at[to])

    if sh < most:

        @pl.when(col == 1)
        def _():
            pl.semaphore_wait(near, 1)
            signal(go_all, core=0)

        @pl.when(col == 0)
        def _():
            pl.semaphore_wait(go_all, 1)

    terms, _ = sums(n, levels, rank)
    sorts = classes_of(terms)
    term = {low - 1: g2[...]}
    for k, h, ch, many, start in reversed(found):
        for l in range(many - 1, -1, -1):
            matrix = s[pl.ds(first_of(in_node, h), h), pl.ds(start + l * ch, ch)].reshape(rank, rank)
            p[l] = p[l] - dot(matrix, term[k])
        term[k - 1] = p[k - 1].astype(bf)
        _, h, ch, _, start = terms[k - 1]
        gs[pl.ds(first_of(in_all, h), h), pl.ds(start, ch)] = term[k - 1].reshape(h, ch, vecs)
    to_g = [slot(2) for _ in sorts]
    to_c = [slot(2) for _ in sorts]
    far_g = {(l, b): slot(2) for l, h, _, _, _ in terms for b in range(log2(group_of[l] // h))}
    for (lo, hi, count), at in reversed(list(zip(sorts, to_g))):
        part = pl.ds(0, count)
        for o in range(hi - 1, max(lo, 1) - 1, -1):
            push(gs.at[in_all ^ o, part], gr.at[col, o, part], me ^ o, at + col, 1)
        if lo == 0:

            @pl.when(col == 0)
            def _():
                push(gs.at[in_all, part], gr.at[0, 0, part], me, at, 1)

        a, b = gs.at[pl.ds(0, hi - lo), part], gs.at[pl.ds(0, hi - max(lo, 1)), part]
        sent.append((0, lambda a=a, at=at: await_bytes(a, ssem.at[at])))
        sent.append((1, lambda b=b, at=at: await_bytes(b, ssem.at[at + 1])))

    got_it.wait()
    out[...] = it[...].astype(f32) - x[...] + dot(xu[:, pl.ds(vecs, rank)], c3)
    come_g2()
    h = min(group_of[low - 1], most)
    ch = rank // h
    share = pl.ds(pl.multiple_of((me & (h - 1)) * ch, 16), ch)
    total = g2[share].astype(f32)
    for o in range(1, h):
        total = total + gr2[pl.ds((o - 1) * ch, ch)].astype(f32)
    c2[share] = total.astype(bf)
    come_c2 = gather(c2, group_of[low - 1])

    @pl.when(col == 1)
    def _():
        for which in (1, 0):
            for (lo, hi, count), at in zip(sorts, to_g):
                begin = max(lo, which)
                await_bytes(gr.at[which, pl.ds(begin, hi - begin), pl.ds(0, count)], rsem.at[at + which])
            for l, h, ch, _, start in terms:
                part = pl.ds(start, ch)
                total = (gs[in_all, part] if which else gr[0, 0, part]).astype(f32)
                for o in range(1, h):
                    total = total + gr[which, o, part].astype(f32)
                for b in range(log2(group_of[l] // h)):
                    gx[l, b, which] = total
                    push(gx.at[l, b, which], gy.at[l, b, which], me ^ (most << b), far_g[l, b] + which).wait_recv()
                    total = total + gy[l, b, which]
                if which:
                    c[in_all, part] = total.astype(bf)
                else:
                    c0[part] = total.astype(bf)
            for (lo, hi, count), at in reversed(list(zip(sorts, to_c))):
                part = pl.ds(0, count)
                share = c.at[in_all, part] if which else c0.at[part]
                for o in range(hi - 1, max(lo, which) - 1, -1):
                    push(share, c.at[in_all, part], me ^ o, at + which, which)

    for l, b in far_g:
        for which in range(2):
            sent.append((1, lambda a=gx.at[l, b, which], at=far_g[l, b] + which: await_bytes(a, ssem.at[at])))
    for (lo, hi, count), at in zip(sorts, to_c):
        a, b = c.at[pl.ds(0, hi - lo), pl.ds(0, count)], c.at[pl.ds(0, hi - max(lo, 1)), pl.ds(0, count)]
        sent.append((1, lambda a=a, at=at: await_bytes(a, ssem.at[at])))
        sent.append((1, lambda b=b, at=at: await_bytes(b, ssem.at[at + 1])))
    ready(low - 1, got_u, in_u)
    come_c2()
    out[...] = out[...] + dot(u[low - 1], c2[...])
    for l in range(low - 2, -1, -1):
        ready(l, got_u, in_u)
    for (lo, hi, count), at in zip(sorts, to_c):
        a, b = c.at[pl.ds(0, hi - lo), pl.ds(0, count)], c.at[pl.ds(0, hi - max(lo, 1)), pl.ds(0, count)]

        @pl.when(col == 0)
        def _():
            await_bytes(a, rsem.at[at])

        @pl.when(col == 1)
        def _():
            await_bytes(b, rsem.at[at + 1])

    whole = jnp.concatenate(
        [c[pl.ds(first_of(in_all, h), h), pl.ds(start, ch)].reshape(rank, vecs) for l, h, ch, _, start in terms])

    num = jnp.zeros((1, vecs), f32)
    den = jnp.zeros((1, vecs), f32)
    blocks = 4
    size = rows // blocks
    for k in range(blocks):
        b = pl.ds(k * size, size)
        updated = out[b] + dot(jnp.concatenate([u[l, b] for l, _, _, _, _ in terms], axis=1), whole)
        out[b] = updated
        num = num + jnp.sum(updated * r[b].astype(f32), axis=0, keepdims=True)
        den = den + jnp.sum(updated * updated, axis=0, keepdims=True)
    st[pl.ds(0, 1)] = num
    st[pl.ds(1, 1)] = den
    at = slot()
    for o in range(most - 1, 0, -1):
        push(st, sg.at[o - 1], me ^ o, at)
    sent.append((None, lambda: await_bytes(sg, ssem.at[at])))
    got_est.wait()
    drain()
    await_bytes(sg, rsem.at[at])
    total = st[...]
    for o in range(1, most):
        total = total + sg[o - 1]
    for b in range(log2(n // most)):
        sx[0, b] = total
        lone(sx.at[0, b], sx.at[1, b], me ^ (most << b)).wait_recv()
        total = total + sx[1, b]
    fun[...] = (est[...] + total[0:1] / (total[1:2] + epsilon)).reshape(vecs)
    drain()


def finish(updated, functional, out, fun, sem):
    size = updated.shape[0] // CUTS
    copies = [
        pltpu.make_async_copy(updated.at[pl.ds(k * size, size)], out.at[pl.ds(k * size, size)], sem.at[k])
        for k in range(CUTS)
    ] + [pltpu.make_async_copy(functional, fun, sem.at[CUTS])]
    for copy in copies:
        copy.start()
    for copy in copies:
        copy.wait()


def per_device(n, iterate, residual, leaf_offset, bases_v, bases_u, estimate):
    rows, vecs = residual.shape
    levels = bases_v.shape[0]
    rank = 2 * bases_v.shape[2]
    width = 2 * leaf_offset.shape[1]
    low = levels - 2
    far = log2(n // min(n, MOST))
    slots = 2 * levels + 10 * low + far * (3 * low + 1) + 8
    found = scratch_of(n, levels, rows, rank, vecs, width)
    anywhere = pl.BlockSpec(memory_space=pl.ANY)
    vmem = pl.BlockSpec(memory_space=pltpu.VMEM)
    args = (iterate, residual, leaf_offset, bases_v, bases_u, estimate.reshape(1, vecs))
    shapes = (
        jax.ShapeDtypeStruct((rows, vecs), jnp.float32),
        jax.ShapeDtypeStruct((vecs,), jnp.float32),
    )
    results = pl.pallas_call(
        functools.partial(kernel, n, [name for name, _, _ in found]),
        out_shape=shapes,
        in_specs=[anywhere] * 6,
        out_specs=(vmem, vmem),
        scratch_shapes=[pltpu.VMEM(shape, kind) for _, kind, shape in found] + [
            pltpu.SemaphoreType.DMA((2 * levels + 2 * (rows // width) + 4,)),
            pltpu.SemaphoreType.DMA((slots,)),
            pltpu.SemaphoreType.DMA((slots,)),
        ] + [pltpu.SemaphoreType.REGULAR] * 5,
        compiler_params=pltpu.CompilerParams(
            collective_id=0, has_side_effects=True, vmem_limit_bytes=44 << 20
        ),
    )(*(pltpu.with_memory_space_constraint(a, pltpu.HBM) for a in args))
    return pl.pallas_call(
        finish,
        out_shape=shapes,
        in_specs=[vmem] * 2,
        out_specs=(anywhere, anywhere),
        scratch_shapes=[pltpu.SemaphoreType.DMA((CUTS + 1,))],
    )(*(pltpu.with_memory_space_constraint(a, pltpu.VMEM) for a in results))


def solution(mesh):
    return jax.shard_map(
        functools.partial(per_device, mesh.shape["rows"]),
        mesh=mesh,
        in_specs=(
            P("rows", "cols"),
            P("rows", "cols"),
            P("rows", "cols"),
            P(None, "rows", "cols"),
            P(None, "rows", "cols"),
            P("cols"),
        ),
        out_specs=(P("rows", "cols"), P("cols")),
        check_vma=False,
    )
```

```python
import functools

import jax
import jax.numpy as jnp
from jax import lax
from jax.experimental import pallas as pl
from jax.experimental.pallas import tpu as pltpu
from jax.sharding import PartitionSpec as P

epsilon = 1e-06
MESH = pl.DeviceIdType.MESH
MOST = 16
CUTS = 1


def log2(value):
    return value.bit_length() - 1


def tdot(a, b):
    return lax.dot_general(a, b, (((0,), (0,)), ((), ())), preferred_element_type=jnp.float32)


def dot(a, b):
    return jnp.dot(a, b, preferred_element_type=jnp.float32)


def shares(n, levels, rank, which, most):
    found, start = [], 0
    for level, many in which:
        h = min(2 ** (levels - 1 - level), most)
        found.append((level, h, rank // h, many, start))
        start += many * (rank // h)
    return found, start


def classes_of(found):
    out, low = [], 0
    for level, h, ch, many, start in reversed(found):
        if h > low:
            out.append((low, h, start + many * ch))
            low = h
    return out


def crosses(n, levels, rank):
    return shares(n, levels, rank, [(k, k) for k in range(1, levels - 2)], MOST)


def sums(n, levels, rank):
    return shares(n, levels, rank, [(l, 1) for l in range(levels - 3)], MOST)


def scratch_of(n, levels, rows, rank, vecs, width):
    half, top = rank // 2, levels - 1
    low = top - 1
    most = min(n, MOST)
    room = max(log2(n // most), 1)
    bf, f32 = jnp.bfloat16, jnp.float32
    sh = min(n // 2, MOST)
    _, cross_rows = crosses(n, levels, rank)
    _, sum_rows = sums(n, levels, rank)
    return [
        ("it", bf, (rows, vecs)),
        ("r", bf, (rows, vecs)),
        ("rp", bf, (rows, vecs)),
        ("leaf", bf, (rows, width)),
        ("v", bf, (levels, rows, rank)),
        ("u", bf, (levels, rows, rank)),
        ("est", f32, (1, vecs)),
        ("x", f32, (rows, vecs)),
        ("xu", bf, (rows, vecs + rank)),
        ("w3", bf, (low, rank, rank)),
        ("p", f32, (low, rank, vecs)),
        ("ps3", bf, (rank, vecs)),
        ("rs3", bf, (rank, vecs)),
        ("g2", bf, (rank, vecs)),
        ("gr2", bf, (rank, vecs)),
        ("c2", bf, (rank, vecs)),
        ("gs", bf, (most, sum_rows, vecs)),
        ("gr", bf, (2, most, sum_rows, vecs)),
        ("c", bf, (most, sum_rows, vecs)),
        ("c0", bf, (sum_rows, vecs)),
        ("gx", f32, (low, room, 2, rank // most, vecs)),
        ("gy", f32, (low, room, 2, rank // most, vecs)),
        ("ws", bf, (sh, cross_rows, half)),
        ("wr", bf, (2, sh, cross_rows, half)),
        ("s", bf, (sh, cross_rows, rank)),
        ("wx", f32, (room, cross_rows, rank)),
        ("wy", f32, (room, cross_rows, rank)),
        ("st", f32, (2, vecs)),
        ("sg", f32, (most - 1, 2, vecs)),
        ("sx", f32, (2, room, 2, vecs)),
    ]


def kernel(n, names, it_h, r_h, leaf_h, v_h, u_h, est_h, out, fun, *refs):
    buf = dict(zip(names, refs))
    lsem, ssem, rsem, hs, go, near, go_all = refs[len(names):]
    it, r, rp, leaf, v, u, est, x, xu = (buf[a] for a in ("it", "r", "rp", "leaf", "v", "u", "est", "x", "xu"))
    w3, p, ps3, rs3, g2, gr2, c2 = (buf[a] for a in ("w3", "p", "ps3", "rs3", "g2", "gr2", "c2"))
    gs, gr, c, c0, gx, gy, ws, wr, s, wx, wy = (
        buf[a] for a in ("gs", "gr", "c", "c0", "gx", "gy", "ws", "wr", "s", "wx", "wy"))
    st, sg, sx = (buf[a] for a in ("st", "sg", "sx"))
    bf, f32 = jnp.bfloat16, jnp.float32
    rows, vecs = r.shape
    levels, _, rank = v.shape
    half = rank // 2
    width = leaf.shape[1]
    lh = width // 2
    leaves = rows // width
    top = levels - 1
    low = top - 1
    most = min(n, MOST)
    sh = min(n // 2, MOST)
    me = lax.axis_index("rows")
    col = lax.axis_index("cols")
    other = 1 - col
    mine = pl.ds(pl.multiple_of(col * half, half), half)
    beside = pl.ds(pl.multiple_of(vecs + col * half, half), half)
    in_node = me & (sh - 1)
    in_all = me & (most - 1)
    group_of = [2 ** (top - l) for l in range(levels)]

    def signal(sem, to=None, core=None):
        device = {} if to is None else {"rows": to}
        if core is not None:
            device["cols"] = core
        pl.semaphore_signal(sem, inc=1, device_id=device, device_id_type=MESH)

    barrier = pltpu.get_barrier_semaphore()
    partners = [1, 2, 3] + [1 << b for b in range(log2(sh), log2(n))]

    @pl.when(col == 1)
    def _():
        signal(barrier, core=0)
        for o in range(sh - 1, 3, -1):
            signal(barrier, me ^ o)

    used = {"l": 0, "s": 0}

    def fetch(src, dst):
        copy = pltpu.make_async_copy(src, dst, lsem.at[used["l"]])
        used["l"] += 1
        copy.start()
        return copy

    got_v, got_u = {}, {}

    def fetch_v(l):
        got_v[l] = fetch(v_h.at[l], v.at[l, :, mine])

    def fetch_u(l):
        got_u[l] = fetch(u_h.at[l], xu.at[:, beside] if l == top - 1 else u.at[l, :, mine])


    @pl.when(col == 0)
    def _():
        pl.semaphore_wait(barrier, 1)
        signal(hs, core=1)

    @pl.when(col == 1)
    def _():
        pl.semaphore_wait(hs, 1)
        for o in partners:
            signal(barrier, me ^ o)

    sent = []

    def drain():
        for where, done in sent:
            if where is None:
                done()
            else:
                pl.when(col == where)(done)
        sent.clear()

    def await_bytes(ref, sem):
        pltpu.make_async_copy(ref, ref, sem).wait()

    def slot(many=1):
        used["s"] += many
        return used["s"] - many

    def push(src, dst, to=None, at=None, core=None):
        at = slot() if at is None else at
        device = {} if to is None else {"rows": to}
        if to is None or core is not None:
            device["cols"] = other if core is None else core
        copy = pltpu.make_async_remote_copy(
            src_ref=src, dst_ref=dst, send_sem=ssem.at[at], recv_sem=rsem.at[at],
            device_id=device, device_id_type=MESH)
        copy.start()
        return copy

    def lone(src, dst, to=None):
        copy = push(src, dst, to)
        sent.append((None, copy.wait_send))
        return copy

    in_v, in_u = {}, {}

    def push_v(l):
        in_v[l] = lone(v_h.at[l], v.at[l, :, mine])

    def push_u(l):
        in_u[l] = lone(u_h.at[l], xu.at[:, beside] if l == top - 1 else u.at[l, :, mine])

    for l in range(low - 1):
        push_v(l)
    for l in range(low - 1):
        fetch_v(l)
        fetch_u(l + 1)
    in_leaf = lone(leaf_h, leaf.at[:, pl.ds(lh, lh)])
    got_r = [fetch(r_h, r)]
    for k in range(leaves):
        for part, which in enumerate((col, other)):
            start = pl.multiple_of(k * width + which * lh, 16)
            got_r.append(fetch(r_h.at[pl.ds(start, lh)], rp.at[pl.ds(k * width + part * lh, lh)]))
    got_leaf = fetch(leaf_h, leaf.at[:, pl.ds(0, lh)])
    fetch_v(top)
    push_v(top)
    fetch_u(top)
    push_u(top)
    fetch_v(top - 1)
    push_v(top - 1)
    fetch_v(low - 1)
    push_v(low - 1)
    fetch_u(top - 1)
    push_u(top - 1)
    fetch_u(0)
    for l in range(low - 1, -1, -1):
        push_u(l)
    got_it = fetch(it_h, it)
    got_est = fetch(est_h, est)

    def ready(l, got, come):
        if l in got:
            got.pop(l).wait()
        come[l].wait_recv()

    def scatter(src, dst, group):
        h = min(group, most)
        ch = rank // h
        j = me & (h - 1)
        at = slot()
        for o in range(h - 1, 0, -1):
            push(src.at[pl.ds(pl.multiple_of((j ^ o) * ch, 16), ch)], dst.at[pl.ds((o - 1) * ch, ch)], me ^ o, at)
        whole = dst.at[pl.ds(0, (h - 1) * ch)]
        sent.append((None, lambda: await_bytes(whole, ssem.at[at])))
        return lambda: await_bytes(whole, rsem.at[at])

    def gather(ref, group):
        h = min(group, most)
        ch = rank // h
        share = pl.ds(pl.multiple_of((me & (h - 1)) * ch, 16), ch)
        at = slot()
        for o in range(h - 1, 0, -1):
            push(ref.at[share], ref.at[share], me ^ o, at)
        whole = ref.at[pl.ds(0, (h - 1) * ch)]
        sent.append((None, lambda: await_bytes(whole, ssem.at[at])))
        return lambda: await_bytes(whole, rsem.at[at])

    def first_of(j, h):
        return j - (j & (h - 1))

    found, _ = crosses(n, levels, rank)
    kinds = classes_of(found)
    to_w = [slot(2) for _ in kinds]
    to_s = [slot() for _ in kinds]
    to_other = [slot() for _ in kinds]
    for k in range(1, low):
        got_u.pop(k).wait()
    for l in range(low - 1):
        ready(l, got_v, in_v)
        below = jnp.concatenate([u[k, :, mine] for k in range(l + 1, low)], axis=1)
        product = tdot(v[l], below).astype(bf)
        for i, (k, h, ch, _, start) in enumerate(found[l:]):
            ws[pl.ds(first_of(in_node, h), h), pl.ds(start + l * ch, ch)] = (
                product[:, i * half:(i + 1) * half].reshape(h, ch, half))
        if l == 0:

            @pl.when(col == 1)
            def _():
                pl.semaphore_wait(barrier, sh - 4 + len(partners))
                signal(go, core=0)

            @pl.when(col == 0)
            def _():
                pl.semaphore_wait(go, 1)

        for (lo, hi, count), at in reversed(list(zip(kinds, to_w))):
            if max(k for k, h, _, _, _ in found if h >= hi) != l + 1:
                continue
            part = pl.ds(0, count)
            for o in range(hi - 1, max(lo, 1) - 1, -1):
                push(ws.at[in_node ^ o, part], wr.at[col, o, part], me ^ o, at + col, 1)
            if lo == 0:

                @pl.when(col == 0)
                def _():
                    push(ws.at[in_node, part], wr.at[0, 0, part], me, at, 1)

            a, b = ws.at[pl.ds(0, hi - lo), part], ws.at[pl.ds(0, hi - max(lo, 1)), part]
            sent.append((0, lambda a=a, at=at: await_bytes(a, ssem.at[at])))
            sent.append((1, lambda b=b, at=at: await_bytes(b, ssem.at[at + 1])))

    for copy in got_r:
        copy.wait()
    got_leaf.wait()
    for k in range(leaves):
        b = pl.ds(k * width, width)
        x[b] = r[b].astype(f32) + dot(leaf[b, pl.ds(0, lh)], rp[pl.ds(k * width, lh)])

    in_leaf.wait_recv()
    for k in range(leaves):
        b = pl.ds(k * width, width)
        x[b] = x[b] + dot(leaf[b, pl.ds(lh, lh)], rp[pl.ds(k * width + lh, lh)])
    ready(top, got_v, in_v)
    narrow = tdot(v[top], x[...].astype(bf)).astype(bf)
    ready(top, got_u, in_u)
    x[...] = x[...] - dot(u[top], narrow)
    xu[:, pl.ds(0, vecs)] = x[...].astype(bf)
    ready(top - 1, got_v, in_v)
    partial = tdot(v[top - 1], xu[:, pl.ds(0, vecs)])
    ps3[...] = partial.astype(bf)
    in_pair = lone(ps3, rs3, me ^ 1)

    far_at = {(k, b): slot() for k, h, _, _, _ in found for b in range(log2(group_of[k] // h))}

    @pl.when(col == 1)
    def _():
        for (lo, hi, count), at in zip(kinds, to_w):
            await_bytes(wr.at[0, pl.ds(lo, hi - lo), pl.ds(0, count)], rsem.at[at])
            await_bytes(wr.at[1, pl.ds(max(lo, 1), hi - max(lo, 1)), pl.ds(0, count)], rsem.at[at + 1])
        for k, h, ch, many, start in found:
            part = pl.ds(start, many * ch)
            first, second = wr[0, 0, part].astype(f32), ws[in_node, part].astype(f32)
            for o in range(1, h):
                first = first + wr[0, o, part].astype(f32)
                second = second + wr[1, o, part].astype(f32)
            for b in range(log2(group_of[k] // h)):
                wx[b, part, pl.ds(0, half)] = first
                wx[b, part, pl.ds(half, half)] = second
                push(wx.at[b, part], wy.at[b, part], me ^ (most << b), far_at[k, b]).wait_recv()
                first = first + wy[b, part, pl.ds(0, half)]
                second = second + wy[b, part, pl.ds(half, half)]
            s[in_node, part, pl.ds(0, half)] = first.astype(bf)
            s[in_node, part, pl.ds(half, half)] = second.astype(bf)
        for (lo, hi, count), at in reversed(list(zip(kinds, to_s))):
            share = s.at[in_node, pl.ds(0, count)]
            for o in range(hi - 1, max(lo, 1) - 1, -1):
                push(share, share, me ^ o, at)
        if sh < most:
            signal(near, me ^ sh)

    for (lo, hi, count), at, to in zip(kinds, to_s, to_other):
        a, b = s.at[pl.ds(0, hi - max(lo, 1)), pl.ds(0, count)], s.at[pl.ds(0, hi - lo), pl.ds(0, count)]
        sent.append((1, lambda a=a, at=at: await_bytes(a, ssem.at[at])))
        sent.append((1, lambda b=b, at=to: await_bytes(b, ssem.at[at])))
    for k, h, ch, many, start in found:
        for b in range(log2(group_of[k] // h)):
            sent.append((1, lambda a=wx.at[b, pl.ds(start, many * ch)], at=far_at[k, b]: await_bytes(a, ssem.at[at])))

    ready(low - 1, got_v, in_v)
    ready(top - 1, got_u, in_u)
    for l in range(low - 1, -1, -1):
        product = tdot(v[l], xu[...])
        p[l] = product[:, :vecs]
        w3[l] = product[:, vecs:].astype(bf)
    in_pair.wait_recv()
    c3 = (partial + rs3[...].astype(f32)).astype(bf)
    p[...] = p[...] - dot(w3[...].reshape(low * rank, rank), c3).reshape(low, rank, vecs)
    g2[...] = p[low - 1].astype(bf)

    come_g2 = scatter(g2, gr2, group_of[low - 1])

    @pl.when(col == 1)
    def _():
        for (lo, hi, count), at, to in zip(kinds, to_s, to_other):
            await_bytes(s.at[pl.ds(0, hi - max(lo, 1)), pl.ds(0, count)], rsem.at[at])
            block = s.at[pl.ds(first_of(in_node, hi) if lo == 0 else first_of(in_node, hi) + lo - (in_node & lo), hi - lo), pl.ds(0, count)]
            push(block, block, me, to, 0)

    @pl.when(col == 0)
    def _():
        for (lo, hi, count), to in zip(kinds, to_other):
            await_bytes(s.at[pl.ds(0, hi - lo), pl.ds(0, count)], rsem.at[to])

    if sh < most:

        @pl.when(col == 1)
        def _():
            pl.semaphore_wait(near, 1)
            signal(go_all, core=0)

        @pl.when(col == 0)
        def _():
            pl.semaphore_wait(go_all, 1)

    terms, _ = sums(n, levels, rank)
    sorts = classes_of(terms)
    term = {low - 1: g2[...]}
    for k, h, ch, many, start in reversed(found):
        for l in range(many - 1, -1, -1):
            matrix = s[pl.ds(first_of(in_node, h), h), pl.ds(start + l * ch, ch)].reshape(rank, rank)
            p[l] = p[l] - dot(matrix, term[k])
        term[k - 1] = p[k - 1].astype(bf)
        _, h, ch, _, start = terms[k - 1]
        gs[pl.ds(first_of(in_all, h), h), pl.ds(start, ch)] = term[k - 1].reshape(h, ch, vecs)
    to_g = [slot(2) for _ in sorts]
    to_c = [slot(2) for _ in sorts]
    far_g = {(l, b): slot(2) for l, h, _, _, _ in terms for b in range(log2(group_of[l] // h))}
    for (lo, hi, count), at in reversed(list(zip(sorts, to_g))):
        part = pl.ds(0, count)
        for o in range(hi - 1, max(lo, 1) - 1, -1):
            push(gs.at[in_all ^ o, part], gr.at[col, o, part], me ^ o, at + col, 1)
        if lo == 0:

            @pl.when(col == 0)
            def _():
                push(gs.at[in_all, part], gr.at[0, 0, part], me, at, 1)

        a, b = gs.at[pl.ds(0, hi - lo), part], gs.at[pl.ds(0, hi - max(lo, 1)), part]
        sent.append((0, lambda a=a, at=at: await_bytes(a, ssem.at[at])))
        sent.append((1, lambda b=b, at=at: await_bytes(b, ssem.at[at + 1])))

    got_it.wait()
    out[...] = it[...].astype(f32) - x[...] + dot(xu[:, pl.ds(vecs, rank)], c3)
    come_g2()
    h = min(group_of[low - 1], most)
    ch = rank // h
    share = pl.ds(pl.multiple_of((me & (h - 1)) * ch, 16), ch)
    total = g2[share].astype(f32)
    for o in range(1, h):
        total = total + gr2[pl.ds((o - 1) * ch, ch)].astype(f32)
    c2[share] = total.astype(bf)
    come_c2 = gather(c2, group_of[low - 1])

    @pl.when(col == 1)
    def _():
        for which in (1, 0):
            for (lo, hi, count), at in zip(sorts, to_g):
                begin = max(lo, which)
                await_bytes(gr.at[which, pl.ds(begin, hi - begin), pl.ds(0, count)], rsem.at[at + which])
            for l, h, ch, _, start in terms:
                part = pl.ds(start, ch)
                total = (gs[in_all, part] if which else gr[0, 0, part]).astype(f32)
                for o in range(1, h):
                    total = total + gr[which, o, part].astype(f32)
                for b in range(log2(group_of[l] // h)):
                    gx[l, b, which] = total
                    push(gx.at[l, b, which], gy.at[l, b, which], me ^ (most << b), far_g[l, b] + which).wait_recv()
                    total = total + gy[l, b, which]
                if which:
                    c[in_all, part] = total.astype(bf)
                else:
                    c0[part] = total.astype(bf)
            for (lo, hi, count), at in reversed(list(zip(sorts, to_c))):
                part = pl.ds(0, count)
                share = c.at[in_all, part] if which else c0.at[part]
                for o in range(hi - 1, max(lo, which) - 1, -1):
                    push(share, c.at[in_all, part], me ^ o, at + which, which)

    for l, b in far_g:
        for which in range(2):
            sent.append((1, lambda a=gx.at[l, b, which], at=far_g[l, b] + which: await_bytes(a, ssem.at[at])))
    for (lo, hi, count), at in zip(sorts, to_c):
        a, b = c.at[pl.ds(0, hi - lo), pl.ds(0, count)], c.at[pl.ds(0, hi - max(lo, 1)), pl.ds(0, count)]
        sent.append((1, lambda a=a, at=at: await_bytes(a, ssem.at[at])))
        sent.append((1, lambda b=b, at=at: await_bytes(b, ssem.at[at + 1])))
    ready(low - 1, got_u, in_u)
    come_c2()
    out[...] = out[...] + dot(u[low - 1], c2[...])
    for l in range(low - 2, -1, -1):
        ready(l, got_u, in_u)
    for (lo, hi, count), at in zip(sorts, to_c):
        a, b = c.at[pl.ds(0, hi - lo), pl.ds(0, count)], c.at[pl.ds(0, hi - max(lo, 1)), pl.ds(0, count)]

        @pl.when(col == 0)
        def _():
            await_bytes(a, rsem.at[at])

        @pl.when(col == 1)
        def _():
            await_bytes(b, rsem.at[at + 1])

    whole = jnp.concatenate(
        [c[pl.ds(first_of(in_all, h), h), pl.ds(start, ch)].reshape(rank, vecs) for l, h, ch, _, start in terms])

    num = jnp.zeros((1, vecs), f32)
    den = jnp.zeros((1, vecs), f32)
    blocks = 4
    size = rows // blocks
    for k in range(blocks):
        b = pl.ds(k * size, size)
        updated = out[b] + dot(jnp.concatenate([u[l, b] for l, _, _, _, _ in terms], axis=1), whole)
        out[b] = updated
        num = num + jnp.sum(updated * r[b].astype(f32), axis=0, keepdims=True)
        den = den + jnp.sum(updated * updated, axis=0, keepdims=True)
    st[pl.ds(0, 1)] = num
    st[pl.ds(1, 1)] = den
    at = slot()
    for o in range(most - 1, 0, -1):
        push(st, sg.at[o - 1], me ^ o, at)
    sent.append((None, lambda: await_bytes(sg, ssem.at[at])))
    got_est.wait()
    drain()
    await_bytes(sg, rsem.at[at])
    total = st[...]
    for o in range(1, most):
        total = total + sg[o - 1]
    for b in range(log2(n // most)):
        sx[0, b] = total
        lone(sx.at[0, b], sx.at[1, b], me ^ (most << b)).wait_recv()
        total = total + sx[1, b]
    fun[...] = (est[...] + total[0:1] / (total[1:2] + epsilon)).reshape(vecs)
    drain()


def finish(updated, functional, out, fun, sem):
    size = updated.shape[0] // CUTS
    copies = [
        pltpu.make_async_copy(updated.at[pl.ds(k * size, size)], out.at[pl.ds(k * size, size)], sem.at[k])
        for k in range(CUTS)
    ] + [pltpu.make_async_copy(functional, fun, sem.at[CUTS])]
    for copy in copies:
        copy.start()
    for copy in copies:
        copy.wait()


def per_device(n, iterate, residual, leaf_offset, bases_v, bases_u, estimate):
    rows, vecs = residual.shape
    levels = bases_v.shape[0]
    rank = 2 * bases_v.shape[2]
    width = 2 * leaf_offset.shape[1]
    low = levels - 2
    far = log2(n // min(n, MOST))
    slots = 2 * levels + 10 * low + far * (3 * low + 1) + 8
    found = scratch_of(n, levels, rows, rank, vecs, width)
    anywhere = pl.BlockSpec(memory_space=pl.ANY)
    vmem = pl.BlockSpec(memory_space=pltpu.VMEM)
    args = (iterate, residual, leaf_offset, bases_v, bases_u, estimate.reshape(1, vecs))
    shapes = (
        jax.ShapeDtypeStruct((rows, vecs), jnp.float32),
        jax.ShapeDtypeStruct((vecs,), jnp.float32),
    )
    results = pl.pallas_call(
        functools.partial(kernel, n, [name for name, _, _ in found]),
        out_shape=shapes,
        in_specs=[anywhere] * 6,
        out_specs=(vmem, vmem),
        scratch_shapes=[pltpu.VMEM(shape, kind) for _, kind, shape in found] + [
            pltpu.SemaphoreType.DMA((2 * levels + 2 * (rows // width) + 4,)),
            pltpu.SemaphoreType.DMA((slots,)),
            pltpu.SemaphoreType.DMA((slots,)),
        ] + [pltpu.SemaphoreType.REGULAR] * 4,
        compiler_params=pltpu.CompilerParams(
            collective_id=0, has_side_effects=True, vmem_limit_bytes=44 << 20
        ),
    )(*(pltpu.with_memory_space_constraint(a, pltpu.HBM) for a in args))
    return pl.pallas_call(
        finish,
        out_shape=shapes,
        in_specs=[vmem] * 2,
        out_specs=(anywhere, anywhere),
        scratch_shapes=[pltpu.SemaphoreType.DMA((CUTS + 1,))],
    )(*(pltpu.with_memory_space_constraint(a, pltpu.VMEM) for a in results))


def solution(mesh):
    return jax.shard_map(
        functools.partial(per_device, mesh.shape["rows"]),
        mesh=mesh,
        in_specs=(
            P("rows", "cols"),
            P("rows", "cols"),
            P("rows", "cols"),
            P(None, "rows", "cols"),
            P(None, "rows", "cols"),
            P("cols"),
        ),
        out_specs=(P("rows", "cols"), P("cols")),
        check_vma=False,
    )
```

```python
import functools

import jax
import jax.numpy as jnp
from jax import lax
from jax.experimental import pallas as pl
from jax.experimental.pallas import tpu as pltpu
from jax.sharding import PartitionSpec as P

epsilon = 1e-06
MESH = pl.DeviceIdType.MESH
MOST = 16
CUTS = 1


def log2(value):
    return value.bit_length() - 1


def tdot(a, b):
    return lax.dot_general(a, b, (((0,), (0,)), ((), ())), preferred_element_type=jnp.float32)


def dot(a, b):
    return jnp.dot(a, b, preferred_element_type=jnp.float32)


def shares(n, levels, rank, which, most):
    found, start = [], 0
    for level, many in which:
        h = min(2 ** (levels - 1 - level), most)
        found.append((level, h, rank // h, many, start))
        start += many * (rank // h)
    return found, start


def classes_of(found):
    out, low = [], 0
    for level, h, ch, many, start in reversed(found):
        if h > low:
            out.append((low, h, start + many * ch))
            low = h
    return out


def crosses(n, levels, rank):
    return shares(n, levels, rank, [(k, k) for k in range(1, levels - 2)], MOST)


def sums(n, levels, rank):
    return shares(n, levels, rank, [(l, 1) for l in range(levels - 3)], MOST)


def scratch_of(n, levels, rows, rank, vecs, width):
    half, top = rank // 2, levels - 1
    low = top - 1
    most = min(n, MOST)
    room = max(log2(n // most), 1)
    bf, f32 = jnp.bfloat16, jnp.float32
    sh = min(n // 2, MOST)
    _, cross_rows = crosses(n, levels, rank)
    _, sum_rows = sums(n, levels, rank)
    return [
        ("it", bf, (rows, vecs)),
        ("r", bf, (rows, vecs)),
        ("rp", bf, (rows, vecs)),
        ("leaf", bf, (rows, width)),
        ("v", bf, (levels, rows, rank)),
        ("u", bf, (levels, rows, rank)),
        ("est", f32, (1, vecs)),
        ("x", f32, (rows, vecs)),
        ("xu", bf, (rows, vecs + rank)),
        ("w3", bf, (low, rank, rank)),
        ("p", f32, (low, rank, vecs)),
        ("ps3", bf, (rank, vecs)),
        ("rs3", bf, (rank, vecs)),
        ("g2", bf, (rank, vecs)),
        ("gr2", bf, (rank, vecs)),
        ("c2", bf, (rank, vecs)),
        ("gs", bf, (most, sum_rows, vecs)),
        ("gr", bf, (2, most, sum_rows, vecs)),
        ("c", bf, (most, sum_rows, vecs)),
        ("c0", bf, (sum_rows, vecs)),
        ("gx", f32, (low, room, 2, rank // most, vecs)),
        ("gy", f32, (low, room, 2, rank // most, vecs)),
        ("ws", bf, (sh, cross_rows, half)),
        ("wr", bf, (2, sh, cross_rows, half)),
        ("s", bf, (sh, cross_rows, rank)),
        ("wx", f32, (room, cross_rows, rank)),
        ("wy", f32, (room, cross_rows, rank)),
        ("st", f32, (2, vecs)),
        ("sg", f32, (most - 1, 2, vecs)),
        ("sx", f32, (2, room, 2, vecs)),
    ]


def kernel(n, names, it_h, r_h, leaf_h, v_h, u_h, est_h, out, fun, *refs):
    buf = dict(zip(names, refs))
    lsem, ssem, rsem, hs, go, go_node, near, go_all = refs[len(names):]
    it, r, rp, leaf, v, u, est, x, xu = (buf[a] for a in ("it", "r", "rp", "leaf", "v", "u", "est", "x", "xu"))
    w3, p, ps3, rs3, g2, gr2, c2 = (buf[a] for a in ("w3", "p", "ps3", "rs3", "g2", "gr2", "c2"))
    gs, gr, c, c0, gx, gy, ws, wr, s, wx, wy = (
        buf[a] for a in ("gs", "gr", "c", "c0", "gx", "gy", "ws", "wr", "s", "wx", "wy"))
    st, sg, sx = (buf[a] for a in ("st", "sg", "sx"))
    bf, f32 = jnp.bfloat16, jnp.float32
    rows, vecs = r.shape
    levels, _, rank = v.shape
    half = rank // 2
    width = leaf.shape[1]
    lh = width // 2
    leaves = rows // width
    top = levels - 1
    low = top - 1
    most = min(n, MOST)
    sh = min(n // 2, MOST)
    me = lax.axis_index("rows")
    col = lax.axis_index("cols")
    other = 1 - col
    mine = pl.ds(pl.multiple_of(col * half, half), half)
    beside = pl.ds(pl.multiple_of(vecs + col * half, half), half)
    in_node = me & (sh - 1)
    in_all = me & (most - 1)
    group_of = [2 ** (top - l) for l in range(levels)]

    def signal(sem, to=None, core=None):
        device = {} if to is None else {"rows": to}
        if core is not None:
            device["cols"] = core
        pl.semaphore_signal(sem, inc=1, device_id=device, device_id_type=MESH)

    barrier = pltpu.get_barrier_semaphore()
    partners = [1] + [1 << b for b in range(log2(sh), log2(n))]

    @pl.when(col == 1)
    def _():
        signal(barrier, core=0)
        for o in range(sh - 1, 1, -1):
            signal(barrier, me ^ o)

    used = {"l": 0, "s": 0}

    def fetch(src, dst):
        copy = pltpu.make_async_copy(src, dst, lsem.at[used["l"]])
        used["l"] += 1
        copy.start()
        return copy

    got_v, got_u = {}, {}

    def fetch_v(l):
        got_v[l] = fetch(v_h.at[l], v.at[l, :, mine])

    def fetch_u(l):
        got_u[l] = fetch(u_h.at[l], xu.at[:, beside] if l == top - 1 else u.at[l, :, mine])


    @pl.when(col == 0)
    def _():
        pl.semaphore_wait(barrier, 1)
        signal(hs, core=1)

    @pl.when(col == 1)
    def _():
        pl.semaphore_wait(hs, 1)
        for o in partners:
            signal(barrier, me ^ o)

    sent = []

    def drain():
        for where, done in sent:
            if where is None:
                done()
            else:
                pl.when(col == where)(done)
        sent.clear()

    def await_bytes(ref, sem):
        pltpu.make_async_copy(ref, ref, sem).wait()

    def slot(many=1):
        used["s"] += many
        return used["s"] - many

    def push(src, dst, to=None, at=None, core=None):
        at = slot() if at is None else at
        device = {} if to is None else {"rows": to}
        if to is None or core is not None:
            device["cols"] = other if core is None else core
        copy = pltpu.make_async_remote_copy(
            src_ref=src, dst_ref=dst, send_sem=ssem.at[at], recv_sem=rsem.at[at],
            device_id=device, device_id_type=MESH)
        copy.start()
        return copy

    def lone(src, dst, to=None):
        copy = push(src, dst, to)
        sent.append((None, copy.wait_send))
        return copy

    in_v, in_u = {}, {}

    def push_v(l):
        in_v[l] = lone(v_h.at[l], v.at[l, :, mine])

    def push_u(l):
        in_u[l] = lone(u_h.at[l], xu.at[:, beside] if l == top - 1 else u.at[l, :, mine])

    for l in range(low - 1):
        push_v(l)
    for l in range(low - 1):
        fetch_v(l)
        fetch_u(l + 1)
    in_leaf = lone(leaf_h, leaf.at[:, pl.ds(lh, lh)])
    got_r = [fetch(r_h, r)]
    for k in range(leaves):
        for part, which in enumerate((col, other)):
            start = pl.multiple_of(k * width + which * lh, 16)
            got_r.append(fetch(r_h.at[pl.ds(start, lh)], rp.at[pl.ds(k * width + part * lh, lh)]))
    got_leaf = fetch(leaf_h, leaf.at[:, pl.ds(0, lh)])
    for l in (top, top - 1):
        fetch_v(l)
        push_v(l)
        fetch_u(l)
        push_u(l)
    fetch_v(low - 1)
    push_v(low - 1)
    fetch_u(0)
    for l in range(low - 1, -1, -1):
        push_u(l)
    got_it = fetch(it_h, it)
    got_est = fetch(est_h, est)

    def ready(l, got, come):
        if l in got:
            got.pop(l).wait()
        come[l].wait_recv()

    def scatter(src, dst, group):
        h = min(group, most)
        ch = rank // h
        j = me & (h - 1)
        at = slot()
        for o in range(h - 1, 0, -1):
            push(src.at[pl.ds(pl.multiple_of((j ^ o) * ch, 16), ch)], dst.at[pl.ds((o - 1) * ch, ch)], me ^ o, at)
        whole = dst.at[pl.ds(0, (h - 1) * ch)]
        sent.append((None, lambda: await_bytes(whole, ssem.at[at])))
        return lambda: await_bytes(whole, rsem.at[at])

    def gather(ref, group):
        h = min(group, most)
        ch = rank // h
        share = pl.ds(pl.multiple_of((me & (h - 1)) * ch, 16), ch)
        at = slot()
        for o in range(h - 1, 0, -1):
            push(ref.at[share], ref.at[share], me ^ o, at)
        whole = ref.at[pl.ds(0, (h - 1) * ch)]
        sent.append((None, lambda: await_bytes(whole, ssem.at[at])))
        return lambda: await_bytes(whole, rsem.at[at])

    def first_of(j, h):
        return j - (j & (h - 1))

    found, _ = crosses(n, levels, rank)
    kinds = classes_of(found)
    to_w = [slot(2) for _ in kinds]
    to_s = [slot() for _ in kinds]
    to_other = [slot() for _ in kinds]
    for k in range(1, low):
        got_u.pop(k).wait()
    for l in range(low - 1):
        ready(l, got_v, in_v)
        below = jnp.concatenate([u[k, :, mine] for k in range(l + 1, low)], axis=1)
        product = tdot(v[l], below).astype(bf)
        for i, (k, h, ch, _, start) in enumerate(found[l:]):
            ws[pl.ds(first_of(in_node, h), h), pl.ds(start + l * ch, ch)] = (
                product[:, i * half:(i + 1) * half].reshape(h, ch, half))
        if l == 0:

            @pl.when(col == 1)
            def _():
                pl.semaphore_wait(barrier, sh - 2 + len(partners))
                signal(go, core=0)

            @pl.when(col == 0)
            def _():
                pl.semaphore_wait(go, 1)

        for (lo, hi, count), at in reversed(list(zip(kinds, to_w))):
            if max(k for k, h, _, _, _ in found if h >= hi) != l + 1:
                continue
            part = pl.ds(0, count)
            for o in range(hi - 1, max(lo, 1) - 1, -1):
                push(ws.at[in_node ^ o, part], wr.at[col, o, part], me ^ o, at + col, 1)
            if lo == 0:

                @pl.when(col == 0)
                def _():
                    push(ws.at[in_node, part], wr.at[0, 0, part], me, at, 1)

            a, b = ws.at[pl.ds(0, hi - lo), part], ws.at[pl.ds(0, hi - max(lo, 1)), part]
            sent.append((0, lambda a=a, at=at: await_bytes(a, ssem.at[at])))
            sent.append((1, lambda b=b, at=at: await_bytes(b, ssem.at[at + 1])))

    for copy in got_r:
        copy.wait()
    got_leaf.wait()
    for k in range(leaves):
        b = pl.ds(k * width, width)
        x[b] = r[b].astype(f32) + dot(leaf[b, pl.ds(0, lh)], rp[pl.ds(k * width, lh)])

    in_leaf.wait_recv()
    for k in range(leaves):
        b = pl.ds(k * width, width)
        x[b] = x[b] + dot(leaf[b, pl.ds(lh, lh)], rp[pl.ds(k * width + lh, lh)])
    ready(top, got_v, in_v)
    narrow = tdot(v[top], x[...].astype(bf)).astype(bf)
    ready(top, got_u, in_u)
    x[...] = x[...] - dot(u[top], narrow)
    xu[:, pl.ds(0, vecs)] = x[...].astype(bf)
    ready(top - 1, got_v, in_v)
    partial = tdot(v[top - 1], xu[:, pl.ds(0, vecs)])
    ps3[...] = partial.astype(bf)
    in_pair = lone(ps3, rs3, me ^ 1)

    far_at = {(k, b): slot() for k, h, _, _, _ in found for b in range(log2(group_of[k] // h))}

    @pl.when(col == 1)
    def _():
        for (lo, hi, count), at in zip(kinds, to_w):
            await_bytes(wr.at[0, pl.ds(lo, hi - lo), pl.ds(0, count)], rsem.at[at])
            await_bytes(wr.at[1, pl.ds(max(lo, 1), hi - max(lo, 1)), pl.ds(0, count)], rsem.at[at + 1])
        for k, h, ch, many, start in found:
            part = pl.ds(start, many * ch)
            first, second = wr[0, 0, part].astype(f32), ws[in_node, part].astype(f32)
            for o in range(1, h):
                first = first + wr[0, o, part].astype(f32)
                second = second + wr[1, o, part].astype(f32)
            for b in range(log2(group_of[k] // h)):
                wx[b, part, pl.ds(0, half)] = first
                wx[b, part, pl.ds(half, half)] = second
                push(wx.at[b, part], wy.at[b, part], me ^ (most << b), far_at[k, b]).wait_recv()
                first = first + wy[b, part, pl.ds(0, half)]
                second = second + wy[b, part, pl.ds(half, half)]
            s[in_node, part, pl.ds(0, half)] = first.astype(bf)
            s[in_node, part, pl.ds(half, half)] = second.astype(bf)
        for (lo, hi, count), at in reversed(list(zip(kinds, to_s))):
            share = s.at[in_node, pl.ds(0, count)]
            for o in range(hi - 1, max(lo, 1) - 1, -1):
                push(share, share, me ^ o, at)
        signal(go_node, core=0)
        if sh < most:
            signal(near, me ^ sh)

    for (lo, hi, count), at, to in zip(kinds, to_s, to_other):
        a, b = s.at[pl.ds(0, hi - max(lo, 1)), pl.ds(0, count)], s.at[pl.ds(0, hi - lo), pl.ds(0, count)]
        sent.append((1, lambda a=a, at=at: await_bytes(a, ssem.at[at])))
        sent.append((1, lambda b=b, at=to: await_bytes(b, ssem.at[at])))
    for k, h, ch, many, start in found:
        for b in range(log2(group_of[k] // h)):
            sent.append((1, lambda a=wx.at[b, pl.ds(start, many * ch)], at=far_at[k, b]: await_bytes(a, ssem.at[at])))

    ready(low - 1, got_v, in_v)
    ready(top - 1, got_u, in_u)
    for l in range(low - 1, -1, -1):
        product = tdot(v[l], xu[...])
        p[l] = product[:, :vecs]
        w3[l] = product[:, vecs:].astype(bf)
    in_pair.wait_recv()
    c3 = (partial + rs3[...].astype(f32)).astype(bf)
    p[...] = p[...] - dot(w3[...].reshape(low * rank, rank), c3).reshape(low, rank, vecs)
    g2[...] = p[low - 1].astype(bf)

    @pl.when(col == 0)
    def _():
        pl.semaphore_wait(go_node, 1)

    come_g2 = scatter(g2, gr2, group_of[low - 1])

    @pl.when(col == 1)
    def _():
        for (lo, hi, count), at, to in zip(kinds, to_s, to_other):
            await_bytes(s.at[pl.ds(0, hi - max(lo, 1)), pl.ds(0, count)], rsem.at[at])
            block = s.at[pl.ds(first_of(in_node, hi) if lo == 0 else first_of(in_node, hi) + lo - (in_node & lo), hi - lo), pl.ds(0, count)]
            push(block, block, me, to, 0)

    @pl.when(col == 0)
    def _():
        for (lo, hi, count), to in zip(kinds, to_other):
            await_bytes(s.at[pl.ds(0, hi - lo), pl.ds(0, count)], rsem.at[to])

    if sh < most:

        @pl.when(col == 1)
        def _():
            pl.semaphore_wait(near, 1)
            signal(go_all, core=0)

        @pl.when(col == 0)
        def _():
            pl.semaphore_wait(go_all, 1)

    terms, _ = sums(n, levels, rank)
    sorts = classes_of(terms)
    term = {low - 1: g2[...]}
    for k, h, ch, many, start in reversed(found):
        matrices = s[pl.ds(first_of(in_node, h), h), pl.ds(start, many * ch)].reshape(many * rank, rank)
        change = dot(matrices, term[k]).reshape(h, many * ch, vecs)
        for l in range(many - 1, -1, -1):
            p[l] = p[l] - change[:, l * ch:(l + 1) * ch].reshape(rank, vecs)
        term[k - 1] = p[k - 1].astype(bf)
        _, h, ch, _, start = terms[k - 1]
        gs[pl.ds(first_of(in_all, h), h), pl.ds(start, ch)] = term[k - 1].reshape(h, ch, vecs)
    to_g = [slot(2) for _ in sorts]
    to_c = [slot(2) for _ in sorts]
    far_g = {(l, b): slot(2) for l, h, _, _, _ in terms for b in range(log2(group_of[l] // h))}
    for (lo, hi, count), at in reversed(list(zip(sorts, to_g))):
        part = pl.ds(0, count)
        for o in range(hi - 1, max(lo, 1) - 1, -1):
            push(gs.at[in_all ^ o, part], gr.at[col, o, part], me ^ o, at + col, 1)
        if lo == 0:

            @pl.when(col == 0)
            def _():
                push(gs.at[in_all, part], gr.at[0, 0, part], me, at, 1)

        a, b = gs.at[pl.ds(0, hi - lo), part], gs.at[pl.ds(0, hi - max(lo, 1)), part]
        sent.append((0, lambda a=a, at=at: await_bytes(a, ssem.at[at])))
        sent.append((1, lambda b=b, at=at: await_bytes(b, ssem.at[at + 1])))

    got_it.wait()
    out[...] = it[...].astype(f32) - x[...] + dot(xu[:, pl.ds(vecs, rank)], c3)
    come_g2()
    h = min(group_of[low - 1], most)
    ch = rank // h
    share = pl.ds(pl.multiple_of((me & (h - 1)) * ch, 16), ch)
    total = g2[share].astype(f32)
    for o in range(1, h):
        total = total + gr2[pl.ds((o - 1) * ch, ch)].astype(f32)
    c2[share] = total.astype(bf)
    come_c2 = gather(c2, group_of[low - 1])

    @pl.when(col == 1)
    def _():
        for which in (1, 0):
            for (lo, hi, count), at in zip(sorts, to_g):
                begin = max(lo, which)
                await_bytes(gr.at[which, pl.ds(begin, hi - begin), pl.ds(0, count)], rsem.at[at + which])
            for l, h, ch, _, start in terms:
                part = pl.ds(start, ch)
                total = (gs[in_all, part] if which else gr[0, 0, part]).astype(f32)
                for o in range(1, h):
                    total = total + gr[which, o, part].astype(f32)
                for b in range(log2(group_of[l] // h)):
                    gx[l, b, which] = total
                    push(gx.at[l, b, which], gy.at[l, b, which], me ^ (most << b), far_g[l, b] + which).wait_recv()
                    total = total + gy[l, b, which]
                if which:
                    c[in_all, part] = total.astype(bf)
                else:
                    c0[part] = total.astype(bf)
            for (lo, hi, count), at in reversed(list(zip(sorts, to_c))):
                part = pl.ds(0, count)
                share = c.at[in_all, part] if which else c0.at[part]
                for o in range(hi - 1, max(lo, which) - 1, -1):
                    push(share, c.at[in_all, part], me ^ o, at + which, which)

    for l, b in far_g:
        for which in range(2):
            sent.append((1, lambda a=gx.at[l, b, which], at=far_g[l, b] + which: await_bytes(a, ssem.at[at])))
    for (lo, hi, count), at in zip(sorts, to_c):
        a, b = c.at[pl.ds(0, hi - lo), pl.ds(0, count)], c.at[pl.ds(0, hi - max(lo, 1)), pl.ds(0, count)]
        sent.append((1, lambda a=a, at=at: await_bytes(a, ssem.at[at])))
        sent.append((1, lambda b=b, at=at: await_bytes(b, ssem.at[at + 1])))
    ready(low - 1, got_u, in_u)
    come_c2()
    out[...] = out[...] + dot(u[low - 1], c2[...])
    for l in range(low - 2, -1, -1):
        ready(l, got_u, in_u)
    for (lo, hi, count), at in zip(sorts, to_c):
        a, b = c.at[pl.ds(0, hi - lo), pl.ds(0, count)], c.at[pl.ds(0, hi - max(lo, 1)), pl.ds(0, count)]

        @pl.when(col == 0)
        def _():
            await_bytes(a, rsem.at[at])

        @pl.when(col == 1)
        def _():
            await_bytes(b, rsem.at[at + 1])

    whole = jnp.concatenate(
        [c[pl.ds(first_of(in_all, h), h), pl.ds(start, ch)].reshape(rank, vecs) for l, h, ch, _, start in terms])

    num = jnp.zeros((1, vecs), f32)
    den = jnp.zeros((1, vecs), f32)
    blocks = 4
    size = rows // blocks
    for k in range(blocks):
        b = pl.ds(k * size, size)
        updated = out[b] + dot(jnp.concatenate([u[l, b] for l, _, _, _, _ in terms], axis=1), whole)
        out[b] = updated
        num = num + jnp.sum(updated * r[b].astype(f32), axis=0, keepdims=True)
        den = den + jnp.sum(updated * updated, axis=0, keepdims=True)
    st[pl.ds(0, 1)] = num
    st[pl.ds(1, 1)] = den
    at = slot()
    for o in range(most - 1, 0, -1):
        push(st, sg.at[o - 1], me ^ o, at)
    sent.append((None, lambda: await_bytes(sg, ssem.at[at])))
    got_est.wait()
    drain()
    await_bytes(sg, rsem.at[at])
    total = st[...]
    for o in range(1, most):
        total = total + sg[o - 1]
    for b in range(log2(n // most)):
        sx[0, b] = total
        lone(sx.at[0, b], sx.at[1, b], me ^ (most << b)).wait_recv()
        total = total + sx[1, b]
    fun[...] = (est[...] + total[0:1] / (total[1:2] + epsilon)).reshape(vecs)
    drain()


def finish(updated, functional, out, fun, sem):
    size = updated.shape[0] // CUTS
    copies = [
        pltpu.make_async_copy(updated.at[pl.ds(k * size, size)], out.at[pl.ds(k * size, size)], sem.at[k])
        for k in range(CUTS)
    ] + [pltpu.make_async_copy(functional, fun, sem.at[CUTS])]
    for copy in copies:
        copy.start()
    for copy in copies:
        copy.wait()


def per_device(n, iterate, residual, leaf_offset, bases_v, bases_u, estimate):
    rows, vecs = residual.shape
    levels = bases_v.shape[0]
    rank = 2 * bases_v.shape[2]
    width = 2 * leaf_offset.shape[1]
    low = levels - 2
    far = log2(n // min(n, MOST))
    slots = 2 * levels + 10 * low + far * (3 * low + 1) + 8
    found = scratch_of(n, levels, rows, rank, vecs, width)
    anywhere = pl.BlockSpec(memory_space=pl.ANY)
    vmem = pl.BlockSpec(memory_space=pltpu.VMEM)
    args = (iterate, residual, leaf_offset, bases_v, bases_u, estimate.reshape(1, vecs))
    shapes = (
        jax.ShapeDtypeStruct((rows, vecs), jnp.float32),
        jax.ShapeDtypeStruct((vecs,), jnp.float32),
    )
    results = pl.pallas_call(
        functools.partial(kernel, n, [name for name, _, _ in found]),
        out_shape=shapes,
        in_specs=[anywhere] * 6,
        out_specs=(vmem, vmem),
        scratch_shapes=[pltpu.VMEM(shape, kind) for _, kind, shape in found] + [
            pltpu.SemaphoreType.DMA((2 * levels + 2 * (rows // width) + 4,)),
            pltpu.SemaphoreType.DMA((slots,)),
            pltpu.SemaphoreType.DMA((slots,)),
        ] + [pltpu.SemaphoreType.REGULAR] * 5,
        compiler_params=pltpu.CompilerParams(
            collective_id=0, has_side_effects=True, vmem_limit_bytes=44 << 20
        ),
    )(*(pltpu.with_memory_space_constraint(a, pltpu.HBM) for a in args))
    return pl.pallas_call(
        finish,
        out_shape=shapes,
        in_specs=[vmem] * 2,
        out_specs=(anywhere, anywhere),
        scratch_shapes=[pltpu.SemaphoreType.DMA((CUTS + 1,))],
    )(*(pltpu.with_memory_space_constraint(a, pltpu.VMEM) for a in results))


def solution(mesh):
    return jax.shard_map(
        functools.partial(per_device, mesh.shape["rows"]),
        mesh=mesh,
        in_specs=(
            P("rows", "cols"),
            P("rows", "cols"),
            P("rows", "cols"),
            P(None, "rows", "cols"),
            P(None, "rows", "cols"),
            P("cols"),
        ),
        out_specs=(P("rows", "cols"), P("cols")),
        check_vma=False,
    )
```
